32 devices in a mesh: ctx: 8 (over y, x, core), head: 4 (over z).
Axes of the slice: x: 2, y: 2, z: 4, core: 2. Of those that a mesh axis runs over, the one named last changes fastest.
Arguments:
- q_lin: bfloat16 [3072, 4096], P('ctx', 'head'), may hold values from -6 to 6
- k_lin: bfloat16 [3072, 4096], P('ctx', 'head'), may hold values from -6 to 6
- v_lin: bfloat16 [3072, 4096], P('ctx', 'head'), may hold values from -33 to 33
- gate_log: float32 [32, 3072], P('head', 'ctx'), may hold values from -0.7 to 0
- lin_gain: float32 [4096], P('head'), may hold values from 0.1 to 1.9
- q_soft: bfloat16 [3072, 4096], P('ctx', 'head'), may hold values from -27 to 27
- k_soft: bfloat16 [3072, 4096], P('ctx', 'head'), may hold values from -27 to 27
- v_soft: bfloat16 [3072, 4096], P('ctx', 'head'), may hold values from -6 to 6
- doc_ids: int32 [3072], P('ctx'), may hold values from 0 to 7, never falling along the last dimension, each value on 1 to 1536 neighbouring positions
Outputs:
- lin_out: bfloat16 [3072, 4096], P('ctx', 'head')
- soft_out: bfloat16 [3072, 4096], P('ctx', 'head')
The draws below stay inside these ranges and needn't reach their ends.
Inputs may be any that keep to these rules, and one draw needn't show every extreme that they name: `doc_ids`: document ids never fall along the tokens; every document holds 1 to 1536 tokens and one holds exactly 1536.
All inputs are finite; a program needn't handle non-finite values.
Results may differ from the reference program's by a relative error of at most 0.0065.
Values may be sent and summed in bfloat16 or wider, within the bound.
No kernel may reach another device: no remote copies, remote signals or barrier semaphores. Data moves between devices by JAX's collectives and lax.ppermute only.
A program may use at most 256 MiB of HBM per device.

```python
import math
import jax
import jax.numpy as jnp
import numpy as np
from jax import lax

ATTENTION_HEADS = 32
HD = 128
TOK_DEV = 384
DOCS = 8
PACKED_TOKENS = 3072
MOST_DOC = 1536


def draw_gate_log(key, part):
    random_keys = jax.random.split(key, 7)
    ranking = jax.random.permutation(random_keys[0], ATTENTION_HEADS)
    fast_count = ATTENTION_HEADS // 2
    fast_heads = ranking < fast_count
    fast_rate = jnp.exp(jax.random.uniform(random_keys[1], (ATTENTION_HEADS,), jnp.float32, math.log(1.0 / 50.0), math.log(1.0 / 30.0)))
    slow_rate = jnp.exp(jax.random.uniform(random_keys[2], (ATTENTION_HEADS,), jnp.float32, math.log(0.2), math.log(0.8))) / MOST_DOC
    decay_rate = jnp.where(fast_heads, fast_rate, slow_rate)
    blocks = PACKED_TOKENS // TOK_DEV
    block_factor = jnp.exp(jax.random.uniform(random_keys[3], (ATTENTION_HEADS, blocks), jnp.float32, math.log(0.5), math.log(2.0)))
    block_factor = jnp.repeat(block_factor, TOK_DEV, axis=1)
    token_factor = jnp.exp(jax.random.uniform(random_keys[4], (ATTENTION_HEADS, PACKED_TOKENS), jnp.float32, math.log(0.6), math.log(1.6)))
    window_mask = jax.random.randint(random_keys[5], (ATTENTION_HEADS, PACKED_TOKENS), 0, PACKED_TOKENS) < 2
    window_length = jax.random.uniform(random_keys[6], (ATTENTION_HEADS, PACKED_TOKENS), jnp.float32, 0.5, 0.8)
    stable_state = -decay_rate[:, None] * block_factor * token_factor
    return jnp.where(window_mask, jnp.log(window_length), stable_state).astype(jnp.float32)


def draw_v_lin(key, part):
    random_keys = jax.random.split(jax.random.fold_in(key, 5), 2)
    ramp_base = 4.0
    values = jnp.clip(jax.random.normal(random_keys[1], (PACKED_TOKENS, ATTENTION_HEADS, HD), jnp.float32), -4.0, 4.0)
    head_place = jnp.arange(ATTENTION_HEADS, dtype=jnp.float32) / (ATTENTION_HEADS - 1)
    head_scale = ramp_base ** head_place * jnp.exp(jax.random.uniform(random_keys[0], (ATTENTION_HEADS,), jnp.float32, math.log(0.85), math.log(1.18)))
    return (values * head_scale[None, :, None]).reshape(PACKED_TOKENS, ATTENTION_HEADS * HD).astype(jnp.bfloat16)


def make_pair(key):
    random_keys = jax.random.split(jax.random.fold_in(key, 11), 2)
    shape = (PACKED_TOKENS, ATTENTION_HEADS, HD)
    queries = jnp.clip(jax.random.normal(random_keys[0], shape, jnp.float32), -4.0, 4.0)
    key_rows = jnp.clip(jax.random.normal(random_keys[1], shape, jnp.float32), -4.0, 4.0)
    return (queries.reshape(PACKED_TOKENS, ATTENTION_HEADS * HD), key_rows.reshape(PACKED_TOKENS, ATTENTION_HEADS * HD))


def draw_q_soft(key, part):
    return make_pair(key)[0].astype(jnp.bfloat16)


def draw_k_soft(key, part):
    return make_pair(key)[1].astype(jnp.bfloat16)


def steps_of(key, shape, cuts, least, top_value):
    def one(dim, blocks):
        heights = jax.random.uniform(jax.random.fold_in(jax.random.fold_in(key, 6), dim), (blocks,), jnp.float32, least / len(cuts), top_value / len(cuts))
        return jnp.repeat(jnp.exp(heights), shape[dim] // blocks).reshape((-1,) + (1,) * (len(shape) - dim - 1))

    loudness = one(*cuts[0])
    for cut in cuts[1:]:
        loudness = loudness * one(*cut)
    return loudness


def length_profile(number_of, total, reach, skew):
    loads = [(1 << 20) // math.isqrt(standing ** skew) + 1 for standing in range(2, number_of + 1)]
    rest, holding = total - reach - (number_of - 1), [1] * (number_of - 1)
    while rest > 0:
        candidates = [i for i in range(number_of - 1) if holding[i] < reach]
        pool, left = sum([loads[i] for i in candidates]), rest
        for i in candidates:
            addition = min(reach - holding[i], max(1, left * loads[i] // pool), rest)
            holding[i] = holding[i] + addition
            rest = rest - addition
    return np.array([reach] + holding)


def uneven(rng, amount, total, limit, slope):
    if amount == 2:
        one = jax.random.randint(rng, (), max(1, total - limit), min(limit, total - 1) + 1)
        return jnp.stack([one, total - one])
    lengths = jnp.asarray(length_profile(amount, total, limit, slope), jnp.int32)
    couples = (amount - 1) // 2
    donor, sink = lengths[1:1 + 2 * couples:2], lengths[2:2 + 2 * couples:2]
    slack = jnp.minimum(donor - 1, limit - sink)
    shifted = jax.random.randint(jax.random.fold_in(rng, 1), (couples,), 0, 1 << 20) % (slack + 1)
    lengths = lengths.at[1:1 + 2 * couples:2].set(donor - shifted).at[2:2 + 2 * couples:2].set(sink + shifted)
    return lengths[jax.random.permutation(jax.random.fold_in(rng, 2), amount)]


def centred(rng, dims, deviation, reach, cuts=(), held_as=jnp.bfloat16):
    values = jax.random.normal(rng, dims, jnp.float32) * deviation
    if len(cuts) > 0:
        values = steps_of(rng, dims, cuts, -0.22, 0.18) * values
    return jnp.clip(values, min=-reach, max=reach).astype(held_as)


def setup_inputs(seed: int = 0) -> dict:
    streams_of = jax.random.split(jax.random.key(seed), 10)
    q_lin = centred(streams_of[0], (PACKED_TOKENS, ATTENTION_HEADS * HD), 1.0, 6.0, ((0, 8), (1, 4)))
    k_lin = centred(streams_of[1], (PACKED_TOKENS, ATTENTION_HEADS * HD), 1.0, 6.0, ((0, 8), (1, 4)))
    v_lin = draw_v_lin(jax.random.fold_in(streams_of[9], 71), 0)
    gate_log = draw_gate_log(jax.random.fold_in(streams_of[9], 71), 0)
    lin_gain = jnp.clip(1.0 + 0.18 * jax.random.normal(streams_of[4], (ATTENTION_HEADS * HD,), jnp.float32), 0.1, 1.9)
    q_soft = draw_q_soft(jax.random.fold_in(streams_of[9], 71), 0)
    k_soft = draw_k_soft(jax.random.fold_in(streams_of[9], 71), 0)
    v_soft = centred(streams_of[7], (PACKED_TOKENS, ATTENTION_HEADS * HD), 1.0, 6.0, ((0, 8), (1, 4)))
    doc_ids = jnp.searchsorted(jnp.cumsum(uneven(streams_of[8], DOCS, PACKED_TOKENS, MOST_DOC, 2)), jnp.arange(PACKED_TOKENS), side="right").astype(jnp.int32)
    return dict(q_lin=q_lin, k_lin=k_lin, v_lin=v_lin, gate_log=gate_log, lin_gain=lin_gain, q_soft=q_soft, k_soft=k_soft, v_soft=v_soft, doc_ids=doc_ids)


highest = lax.Precision.HIGHEST
epsilon = 1e-05
span_rows = 128

def linear_block(carried_in, inputs):
    lin_state, prev_doc = carried_in
    queries, key_heads, value_heads, gates, doc_block = inputs
    cumulated = jnp.cumsum(gates, axis=1)
    positions = jnp.arange(doc_block.shape[0], dtype=jnp.int32)
    same_doc = (doc_block[:, None] == doc_block[None, :]) & (positions[:, None] >= positions[None, :])
    spread = jnp.minimum(cumulated[:, :, None] - cumulated[:, None, :], 0.0)
    decay_table = jnp.where(same_doc[None], jnp.exp(spread), 0.0)
    scores = jnp.einsum('hte,hse->hts', queries, key_heads, precision=highest) * decay_table
    local_term = jnp.einsum('hts,hse->hte', scores, value_heads, precision=highest)
    carried = jnp.where(doc_block[None, :] == prev_doc, jnp.exp(cumulated), 0.0)
    incoming_term = jnp.einsum('hte,hef->htf', queries, lin_state, precision=highest) * carried[:, :, None]
    end_doc = doc_block[-1]
    end_weight = jnp.where(doc_block[None, :] == end_doc, jnp.exp(cumulated[:, -1:] - cumulated), 0.0)
    fresh_state = jnp.einsum('hse,hsf->hef', key_heads * end_weight[:, :, None], value_heads, precision=highest)
    kept_share = jnp.where(prev_doc == end_doc, jnp.exp(cumulated[:, -1]), 0.0)
    return ((kept_share[:, None, None] * lin_state + fresh_state, end_doc), local_term + incoming_term)

def reference(q_lin, k_lin, v_lin, gate_log, lin_gain, q_soft, k_soft, v_soft, doc_ids):
    token_count = q_lin.shape[0]
    span_count = token_count // span_rows

    def to_spans(array):
        return array.astype(jnp.float32).reshape(span_count, span_rows, ATTENTION_HEADS, HD).transpose(0, 2, 1, 3)
    gate_spans = gate_log.reshape(ATTENTION_HEADS, span_count, span_rows).transpose(1, 0, 2)
    doc_spans = doc_ids.reshape(span_count, span_rows)
    start_state = (jnp.zeros((ATTENTION_HEADS, HD, HD), jnp.float32), jnp.array(-1, dtype=jnp.int32))
    closing, spans = lax.scan(linear_block, start_state, (to_spans(q_lin), to_spans(k_lin), to_spans(v_lin), gate_spans, doc_spans))
    raw_output = spans.transpose(0, 2, 1, 3).reshape(token_count, ATTENTION_HEADS * HD)
    mean_square = lax.optimization_barrier(jnp.mean(raw_output * raw_output, axis=1, keepdims=True))
    lin_out = (raw_output * lax.rsqrt(mean_square + epsilon) * lin_gain[None, :]).astype(jnp.bfloat16)
    query_blocks = token_count // span_rows
    q_heads = q_soft.reshape(token_count, ATTENTION_HEADS, HD).transpose(1, 0, 2)
    k_heads = k_soft.reshape(token_count, ATTENTION_HEADS, HD).transpose(1, 0, 2)
    v_heads = v_soft.reshape(token_count, ATTENTION_HEADS, HD).transpose(1, 0, 2)
    key_pos = jnp.arange(token_count, dtype=jnp.int32)
    score_scale = HD ** (-0.5)

    def soft_item(item_index):
        head_index = item_index // query_blocks
        first_row = (item_index % query_blocks * span_rows).astype(jnp.int32)
        queries = lax.dynamic_slice_in_dim(q_heads[head_index], first_row, span_rows, 0)
        query_docs = lax.dynamic_slice_in_dim(doc_ids, first_row, span_rows, 0)
        query_pos = first_row + jnp.arange(span_rows, dtype=jnp.int32)
        scores = jnp.dot(queries, k_heads[head_index].T, preferred_element_type=jnp.float32) * score_scale
        allowed = (key_pos[None, :] <= query_pos[:, None]) & (doc_ids[None, :] == query_docs[:, None])
        row_max = lax.optimization_barrier(jnp.max(jnp.where(allowed, scores, -jnp.inf), axis=1, keepdims=True))
        weights = jnp.where(allowed, jnp.exp(scores - row_max), 0.0)
        row_total = lax.optimization_barrier(jnp.sum(weights, axis=1, keepdims=True))
        mixed = jnp.dot(weights.astype(jnp.bfloat16), v_heads[head_index], preferred_element_type=jnp.float32)
        return (mixed / row_total).astype(jnp.bfloat16)
    soft_blocks = lax.map(soft_item, jnp.arange(ATTENTION_HEADS * query_blocks, dtype=jnp.int32))
    soft_out = soft_blocks.reshape(ATTENTION_HEADS, token_count, HD).transpose(1, 0, 2).reshape(token_count, ATTENTION_HEADS * HD)
    return (lin_out, soft_out)
```

```python
import functools
import math

import jax
import jax.numpy as jnp
from jax import lax
from jax.experimental import pallas as pl
from jax.experimental.pallas import tpu as pltpu
from jax.sharding import PartitionSpec as P

EPSILON = 1e-05
MASKED = -1e30
LANES = 128
META = 16
TILE = 256
F32 = jnp.float32
BF16 = jnp.bfloat16
HIGHEST = lax.Precision.HIGHEST
VMEM_LIMIT = 48 << 20


def nt_dot(a, b, precision=None):
    return lax.dot_general(
        a, b, (((1,), (1,)), ((), ())), precision=precision, preferred_element_type=F32
    )


def column_of(row):
    return jnp.transpose(jnp.broadcast_to(row, (LANES, LANES)))


def cumulate(gates):
    rows = gates.shape[1]
    upper = lax.broadcasted_iota(jnp.int32, (rows, rows), 0) <= lax.broadcasted_iota(
        jnp.int32, (rows, rows), 1
    )
    return jnp.dot(gates, jnp.where(upper, 1.0, 0.0), precision=HIGHEST, preferred_element_type=F32)


def pack_kernel(q_ref, k_ref, v_ref, doc_ref, out_ref):
    rows = q_ref.shape[0]
    out_ref[0, 0:rows] = q_ref[...]
    out_ref[0, rows : 2 * rows] = k_ref[...]
    out_ref[0, 2 * rows : 3 * rows] = v_ref[...]
    doc = doc_ref[...].astype(F32)
    line = lax.broadcasted_iota(jnp.int32, (META, LANES), 0)
    block = jnp.zeros((META, LANES), F32)
    for i in range(rows // LANES):
        block = jnp.where(line == i, doc[:, i * LANES : (i + 1) * LANES], block)
    out_ref[0, 3 * rows : 3 * rows + META] = block.astype(BF16)


def pack(q, k, v, doc_row, heads):
    rows = q.shape[0]
    total = 3 * rows + META
    block = pl.BlockSpec((rows, LANES), lambda h: (0, h))
    return pl.pallas_call(
        pack_kernel,
        grid=(heads,),
        in_specs=[block, block, block, pl.BlockSpec((1, rows), lambda h: (0, 0))],
        out_specs=pl.BlockSpec((1, total, LANES), lambda h: (h, 0, 0)),
        out_shape=jax.ShapeDtypeStruct((heads, total, LANES), BF16),
        cost_estimate=pl.CostEstimate(
            flops=0, bytes_accessed=4 * heads * total * LANES, transcendentals=0
        ),
        name="pack",
    )(q, k, v, doc_row)


def attend_kernel(rows, window, x_ref, o_ref, s_ref):
    parts = x_ref.shape[0]
    tokens = parts * rows
    per = rows // LANES
    factor = LANES ** (-0.5) * math.log2(math.e)
    docs = x_ref[:, 3 * rows : 3 * rows + META, :].astype(F32)
    used = lax.broadcasted_iota(jnp.int32, docs.shape, 1) < per
    starts = [
        jnp.sum(jnp.where(used & (docs < d), 1, 0).astype(jnp.int32)) for d in range(1, 8)
    ]

    def chunk(which, g):
        offset = pl.multiple_of(which * rows + (g % per) * LANES, LANES)
        return x_ref[g // per, pl.ds(offset, LANES), :]

    def tile(which, t):
        n = TILE // LANES
        return jnp.concatenate([chunk(which, t * n + j) for j in range(n)], axis=0)

    wide = (TILE, LANES)
    ones = jnp.ones(wide, BF16)
    lane = lax.broadcasted_iota(jnp.int32, wide, 1)
    sub = lax.broadcasted_iota(jnp.int32, wide, 0)

    def body(i, carry):
        first = i * TILE
        queries = tile(0, i)
        qpos = first + sub
        begin = jnp.zeros(wide, jnp.int32)
        low = 0
        for s in starts:
            begin = jnp.where(qpos >= s, s, begin)
            low = jnp.where(first >= s, s, low)
        count = i - low // TILE + 1

        def run(n):
            top = jnp.full(wide, MASKED, F32)
            for j in range(n):
                t = i - (n - 1) + j
                s = nt_dot(queries, tile(1, t))
                pieces = []
                for c in range(TILE // LANES):
                    kpos = t * TILE + c * LANES + lane
                    ok = kpos >= begin
                    if j == n - 1:
                        ok = ok & (kpos <= qpos)
                    piece = jnp.where(ok, s[:, c * LANES : (c + 1) * LANES], MASKED)
                    top = jnp.maximum(top, piece)
                    pieces.append(piece)
                s_ref[j] = jnp.concatenate(pieces, axis=1)
            row_max = jnp.max(top, axis=1, keepdims=True)
            total = jnp.zeros((TILE, 2 * LANES), F32)
            for j in range(n):
                t = i - (n - 1) + j
                w = jnp.exp2((s_ref[j] - row_max) * factor).astype(BF16)
                total += jnp.dot(
                    w, jnp.concatenate([tile(2, t), ones], axis=1), preferred_element_type=F32
                )
            o_ref[pl.ds(pl.multiple_of(first, TILE), TILE), :] = (
                total[:, :LANES] / total[:, LANES:]
            ).astype(BF16)

        for n in range(1, window + 1):
            pl.when(count == n)(functools.partial(run, n))
        return carry

    lax.fori_loop(0, tokens // TILE, body, 0)


def attend(x, rows, longest):
    parts, total, _ = x.shape
    tokens = parts * rows
    window = min((longest - 1 + TILE - 1) // TILE + 1, tokens // TILE)
    return pl.pallas_call(
        functools.partial(attend_kernel, rows, window),
        in_specs=[pl.BlockSpec(memory_space=pltpu.VMEM)],
        out_specs=pl.BlockSpec(memory_space=pltpu.VMEM),
        out_shape=jax.ShapeDtypeStruct((tokens, LANES), BF16),
        scratch_shapes=[pltpu.VMEM((window, TILE, TILE), F32)],
        cost_estimate=pl.CostEstimate(
            flops=2 * tokens * longest * LANES * 2,
            bytes_accessed=2 * (x.size + tokens * LANES),
            transcendentals=tokens * longest,
        ),
        compiler_params=pltpu.CompilerParams(vmem_limit_bytes=VMEM_LIMIT),
        name="attend",
    )(x)


def attend_gathered(q, k, v, doc_ids, heads):
    rows = q.shape[0]
    keys = lax.all_gather(k, "ctx", axis=0, tiled=True)
    values = lax.all_gather(v, "ctx", axis=0, tiled=True)
    docs = lax.all_gather(doc_ids, "ctx", axis=0, tiled=True)
    position = lax.axis_index("ctx") * rows + jnp.arange(rows)
    allowed = (jnp.arange(docs.shape[0])[None, :] <= position[:, None]) & (
        docs[None, :] == doc_ids[:, None]
    )

    def one(h):
        queries, head_keys, head_values = (
            lax.dynamic_slice_in_dim(a, h * LANES, LANES, 1) for a in (q, keys, values)
        )
        scores = jnp.where(allowed, nt_dot(queries, head_keys) * LANES ** (-0.5), MASKED)
        weights = jnp.exp(scores - jnp.max(scores, axis=1, keepdims=True))
        mixed = jnp.dot(weights.astype(BF16), head_values, preferred_element_type=F32)
        return (mixed / jnp.sum(weights, axis=1, keepdims=True)).astype(BF16)

    return lax.map(one, jnp.arange(heads)).transpose(1, 0, 2).reshape(rows, heads * LANES)


def meta_block(first, last, factors):
    line = lax.broadcasted_iota(jnp.int32, (META, LANES), 0)
    block = jnp.zeros((META, LANES), F32)
    n = len(factors)
    for i, f in enumerate(factors):
        high = f.astype(BF16).astype(F32)
        block = jnp.where(line == i, high, block)
        block = jnp.where(line == n + i, f - high, block)
    block = jnp.where(line == 2 * n, first, block)
    block = jnp.where(line == 2 * n + 1, last, block)
    return block.astype(BF16)


def read_meta(ref, n):
    block = ref[n * LANES : n * LANES + META, :].astype(F32)
    factors = [block[i : i + 1] + block[n + i : n + i + 1] for i in range(n)]
    return block[2 * n : 2 * n + 1], block[2 * n + 1 : 2 * n + 2], factors


def local_state_kernel(half, core_ref, gate_ref, doc_ref, k_ref, v_ref, mine_ref, other_ref, w_ref, f_ref):
    i = pl.program_id(0)
    rows = k_ref.shape[0]
    core = core_ref[0]

    @pl.when(i == 0)
    def _():
        cumulated = cumulate(gate_ref[...])
        last = cumulated[:, rows - 1 : rows]
        doc = doc_ref[...]
        end = doc[:, rows - 1 : rows]
        w_ref[...] = jnp.where(doc == end, jnp.exp(last - cumulated), 0.0)
        whole = jnp.where(doc[:, 0:1] == end, 1.0, 0.0)
        f_ref[...] = jnp.broadcast_to(jnp.exp(last) * whole, f_ref.shape)
        first_doc = jnp.broadcast_to(doc[:, 0:1].astype(F32), (1, LANES))
        last_doc = jnp.broadcast_to(end.astype(F32), (1, LANES))
        for ref, base in ((mine_ref, core * half), (other_ref, (1 - core) * half)):
            factors = [f_ref[pl.ds(base + j, 1), :] for j in range(half)]
            ref[half * LANES : half * LANES + META, :] = meta_block(first_doc, last_doc, factors)

    head = lax.rem(core * half + i, 2 * half)
    weighted = jnp.transpose(k_ref[...].astype(F32)) * w_ref[pl.ds(head, 1), :]
    state = jnp.dot(weighted.astype(BF16), v_ref[...], preferred_element_type=F32).astype(BF16)
    place = pl.ds(pl.multiple_of(lax.rem(i, half) * LANES, LANES), LANES)

    @pl.when(i < half)
    def _():
        mine_ref[place, :] = state

    @pl.when(i >= half)
    def _():
        other_ref[place, :] = state


def local_state(k, v, gates, doc_row, core, heads):
    rows = k.shape[0]
    half = heads // 2
    block = pl.BlockSpec((rows, LANES), lambda i, c: (0, lax.rem(c[0] * half + i, heads)))
    fixed = lambda i, c: (0, 0)
    sent = (half * LANES + META, LANES)
    return pl.pallas_call(
        functools.partial(local_state_kernel, half),
        grid_spec=pltpu.PrefetchScalarGridSpec(
            num_scalar_prefetch=1,
            grid=(heads,),
            in_specs=[
                pl.BlockSpec((heads, rows), fixed),
                pl.BlockSpec((1, rows), fixed),
                block,
                block,
            ],
            out_specs=[pl.BlockSpec(sent, fixed), pl.BlockSpec(sent, fixed)],
            scratch_shapes=[pltpu.VMEM((heads, rows), F32), pltpu.VMEM((heads, LANES), F32)],
        ),
        out_shape=[jax.ShapeDtypeStruct(sent, BF16)] * 2,
        cost_estimate=pl.CostEstimate(
            flops=2 * heads * rows * LANES * LANES,
            bytes_accessed=4 * heads * rows * LANES + 4 * heads * LANES * LANES,
            transcendentals=heads * rows,
        ),
        name="local_state",
    )(core, gates, doc_row, k, v)


def join(n, early, late, out_ref):
    early_first, early_last, early_factor = read_meta(early, n)
    late_first, late_last, late_factor = read_meta(late, n)
    linked = (early_last == late_first) | (early_last < 0) | (late_first < 0)
    link = jnp.where(linked, 1.0, 0.0)
    first = jnp.where(early_first < 0, late_first, early_first)
    last = jnp.where(late_last < 0, early_last, late_last)
    for i in range(n):
        at = slice(i * LANES, (i + 1) * LANES)
        out_ref[at, :] = (
            late[at, :].astype(F32) + (late_factor[i] * link) * early[at, :].astype(F32)
        ).astype(BF16)
    factors = [early_factor[i] * late_factor[i] * link for i in range(n)]
    out_ref[n * LANES : n * LANES + META, :] = meta_block(first, last, factors)


def set_neutral(n, ref):
    ref[0 : n * LANES, :] = jnp.zeros((n * LANES, LANES), BF16)
    away = jnp.full((1, LANES), -1.0, F32)
    ref[n * LANES : n * LANES + META, :] = meta_block(away, away, [jnp.ones((1, LANES), F32)] * n)


def join_pair_kernel(n, flag_ref, mine_ref, came_ref, out_ref):
    @pl.when(flag_ref[0] == 0)
    def _():
        join(n, mine_ref, came_ref, out_ref)

    @pl.when(flag_ref[0] != 0)
    def _():
        join(n, came_ref, mine_ref, out_ref)


def join_pair(mine, came, flag, n):
    return pl.pallas_call(
        functools.partial(join_pair_kernel, n),
        in_specs=[pl.BlockSpec(memory_space=pltpu.SMEM)]
        + [pl.BlockSpec(memory_space=pltpu.VMEM)] * 2,
        out_specs=pl.BlockSpec(memory_space=pltpu.VMEM),
        out_shape=jax.ShapeDtypeStruct(mine.shape, BF16),
        cost_estimate=pl.CostEstimate(
            flops=2 * mine.size, bytes_accessed=6 * mine.size, transcendentals=0
        ),
        name="join_pair",
    )(flag, mine, came)


def before_kernel(n, bits, flag_ref, mine_ref, mate_ref, *refs):
    came, (keep_ref, send_ref), (a_ref, b_ref) = refs[:bits], refs[bits : bits + 2], refs[bits + 2 :]
    set_neutral(n, a_ref)
    now, spare = a_ref, b_ref
    for b in range(bits):
        late = flag_ref[b + 1] != 0

        def put(source=now, target=spare):
            target[...] = source[...]

        def add(other=came[b], source=now, target=spare):
            join(n, other, source, target)

        pl.when(late)(add)
        pl.when(jnp.logical_not(late))(put)
        now, spare = spare, now

    @pl.when(flag_ref[0] == 0)
    def _():
        keep_ref[...] = now[...]
        join(n, now, mine_ref, send_ref)

    @pl.when(flag_ref[0] != 0)
    def _():
        join(n, now, mate_ref, keep_ref)
        send_ref[...] = now[...]


def before(mine, mate, came, flags, n):
    return pl.pallas_call(
        functools.partial(before_kernel, n, len(came)),
        in_specs=[pl.BlockSpec(memory_space=pltpu.SMEM)]
        + [pl.BlockSpec(memory_space=pltpu.VMEM)] * (2 + len(came)),
        out_specs=[pl.BlockSpec(memory_space=pltpu.VMEM)] * 2,
        out_shape=[jax.ShapeDtypeStruct(mine.shape, BF16)] * 2,
        scratch_shapes=[pltpu.VMEM(mine.shape, BF16)] * 2,
        cost_estimate=pl.CostEstimate(
            flops=4 * mine.size, bytes_accessed=12 * mine.size, transcendentals=0
        ),
        name="before",
    )(flags, mine, mate, *came)


def carried_in(mine, other, place, size, n):
    def swap(x, bit):
        return lax.ppermute(x, "ctx", [(i, i ^ (1 << bit)) for i in range(size)])

    bits = size.bit_length() - 1
    flags = (place >> jnp.arange(bits)) & 1
    mate = swap(other, 0)
    block = join_pair(mine, mate, flags[0:1], n)
    came = []
    for b in range(1, bits):
        came.append(swap(block, b))
        if b < bits - 1:
            block = join_pair(block, came[-1], flags[b : b + 1], n)
    keep, send = before(mine, mate, came, flags, n)
    return keep, swap(send, 0)


def linear_kernel(half, core_ref, gate_ref, doc_ref, q_ref, k_ref, v_ref, keep_ref, came_ref, raw_ref, square_ref, cum_ref, bias_ref, doc_col_ref, sum_ref):
    h = pl.program_id(0)
    rows = q_ref.shape[0]
    count = rows // LANES

    @pl.when(h == 0)
    def _():
        cum_ref[...] = cumulate(gate_ref[...])
        doc = doc_ref[...].astype(F32)
        for a in range(count):
            column = column_of(doc[:, a * LANES : (a + 1) * LANES])
            doc_col_ref[a * LANES : (a + 1) * LANES, :] = column
            for b in range(a + 1):
                ok = column == doc[:, b * LANES : (b + 1) * LANES]
                if a == b:
                    ok = ok & (
                        lax.broadcasted_iota(jnp.int32, (LANES, LANES), 0)
                        >= lax.broadcasted_iota(jnp.int32, (LANES, LANES), 1)
                    )
                bias_ref[a * LANES : (a + 1) * LANES, b * LANES : (b + 1) * LANES] = jnp.where(
                    ok, 0.0, MASKED
                )
        sum_ref[...] = jnp.zeros_like(sum_ref)

    row = cum_ref[pl.ds(h, 1), :]
    own = (h // half) == core_ref[0]
    place = pl.ds(pl.multiple_of(lax.rem(h, half) * LANES, LANES), LANES)
    state = jnp.where(own, keep_ref[place, :].astype(F32), came_ref[place, :].astype(F32)).astype(BF16)
    _, before_doc, _ = read_meta(keep_ref, half)
    for a in range(count):
        at = slice(a * LANES, (a + 1) * LANES)
        width = (a + 1) * LANES
        column = column_of(row[:, at])
        q = q_ref[at, :]
        scores = nt_dot(q, k_ref[0:width, :])
        decay = jnp.concatenate(
            [
                jnp.exp(
                    jnp.minimum(column - row[:, b * LANES : (b + 1) * LANES], 0.0)
                    + bias_ref[at, b * LANES : (b + 1) * LANES]
                )
                for b in range(a + 1)
            ],
            axis=1,
        )
        raw = jnp.dot((scores * decay).astype(BF16), v_ref[0:width, :], preferred_element_type=F32)
        carried = jnp.where(doc_col_ref[at, :] == before_doc, jnp.exp(column), 0.0)
        raw = raw + jnp.dot(q, state, preferred_element_type=F32) * carried
        raw_ref[at, :] = raw
        sum_ref[at, :] += raw * raw

    @pl.when(h == pl.num_programs(0) - 1)
    def _():
        square_ref[...] = nt_dot(jnp.ones((8, LANES), F32), sum_ref[...], HIGHEST)


def linear(q, k, v, gates, doc_row, keep, came, core, heads):
    rows = q.shape[0]
    half = heads // 2
    block = pl.BlockSpec((rows, LANES), lambda h, c: (0, h))
    fixed = lambda h, c: (0, 0)
    return pl.pallas_call(
        functools.partial(linear_kernel, half),
        grid_spec=pltpu.PrefetchScalarGridSpec(
            num_scalar_prefetch=1,
            grid=(heads,),
            in_specs=[
                pl.BlockSpec((heads, rows), fixed),
                pl.BlockSpec((1, rows), fixed),
                block,
                block,
                block,
                pl.BlockSpec(keep.shape, fixed),
                pl.BlockSpec(came.shape, fixed),
            ],
            out_specs=[block, pl.BlockSpec((8, rows), fixed)],
            scratch_shapes=[
                pltpu.VMEM((heads, rows), F32),
                pltpu.VMEM((rows, rows), F32),
                pltpu.VMEM((rows, LANES), F32),
                pltpu.VMEM((rows, LANES), F32),
            ],
        ),
        out_shape=[
            jax.ShapeDtypeStruct((rows, heads * LANES), F32),
            jax.ShapeDtypeStruct((8, rows), F32),
        ],
        cost_estimate=pl.CostEstimate(
            flops=4 * heads * rows * rows * LANES,
            bytes_accessed=10 * heads * rows * LANES,
            transcendentals=heads * rows * rows,
        ),
        name="linear",
    )(core, gates, doc_row, q, k, v, keep, came)


def on_device(size, head_parts, q_lin, k_lin, v_lin, gate_log, lin_gain, q_soft, k_soft, v_soft, doc_ids):
    heads, rows = gate_log.shape
    place = lax.axis_index("ctx")
    core = (place & 1)[None]
    doc_row = doc_ids.reshape(1, rows)

    whole_heads = heads == size
    if whole_heads:
        sent = pack(q_soft, k_soft, v_soft, doc_row, heads)
        held = lax.all_to_all(sent, "ctx", split_axis=0, concat_axis=0, tiled=True)

    mine, other = local_state(k_lin, v_lin, gate_log, doc_row, core, heads)
    keep, came = carried_in(mine, other, place, size, heads // 2)
    raw, square = linear(q_lin, k_lin, v_lin, gate_log, doc_row, keep, came, core, heads)

    if whole_heads:
        mixed = attend(held, rows, rows * size // 2)
        mixed = lax.all_to_all(
            mixed.reshape(size, rows, LANES), "ctx", split_axis=0, concat_axis=0, tiled=True
        )
        soft_out = mixed.transpose(1, 0, 2).reshape(rows, heads * LANES)
    else:
        soft_out = attend_gathered(q_soft, k_soft, v_soft, doc_ids, heads)

    own = square[0]
    total = own
    for d in range(1, head_parts):
        total = total + lax.ppermute(own, "head", [(i, (i + d) % head_parts) for i in range(head_parts)])
    scale = lax.rsqrt(total / (heads * head_parts * LANES) + EPSILON)
    lin_out = (raw * scale[:, None] * lin_gain[None, :]).astype(BF16)
    return lin_out, soft_out


def solution(mesh):
    split = P("ctx", "head")
    in_specs = (split, split, split, P("head", "ctx"), P("head"), split, split, split, P("ctx"))
    return jax.shard_map(
        functools.partial(on_device, mesh.shape["ctx"], mesh.shape["head"]),
        mesh=mesh,
        in_specs=in_specs,
        out_specs=(split, split),
        check_vma=False,
    )
```

```python
import functools
import math

import jax
import jax.numpy as jnp
from jax import lax
from jax.experimental import pallas as pl
from jax.experimental.pallas import tpu as pltpu
from jax.sharding import PartitionSpec as P

EPSILON = 1e-05
MASKED = -1e30
LANES = 128
META = 16
DOC_LINE = 4
LAST_DOC_ID = 7
TILE = 256
F32 = jnp.float32
BF16 = jnp.bfloat16
HIGHEST = lax.Precision.HIGHEST
IN_VMEM = pl.BlockSpec(memory_space=pltpu.VMEM)
PARAMS = pltpu.CompilerParams(vmem_limit_bytes=48 << 20)


def nt_dot(a, b, precision=None):
    return lax.dot_general(
        a, b, (((1,), (1,)), ((), ())), precision=precision, preferred_element_type=F32
    )


def head_at(h):
    return slice(h * LANES, (h + 1) * LANES)


def column_of(row):
    return jnp.transpose(jnp.broadcast_to(row, (LANES, LANES)))


def three_parts(x):
    a = x.astype(BF16).astype(F32)
    b = (x - a).astype(BF16).astype(F32)
    return a, b, x - a - b


def cumulate(gates):
    heads, rows = gates.shape
    lower = lax.broadcasted_iota(jnp.int32, (rows, rows), 0) <= lax.broadcasted_iota(
        jnp.int32, (rows, rows), 1
    )
    parts = jnp.concatenate([*three_parts(gates), jnp.zeros_like(gates)], axis=0).astype(BF16)
    sums = jnp.dot(parts, jnp.where(lower, 1.0, 0.0).astype(BF16), preferred_element_type=F32)
    return sums[:heads] + sums[heads : 2 * heads] + sums[2 * heads : 3 * heads]


def columns(x):
    heads, rows = x.shape
    filler = jnp.zeros((LANES - 3 * heads, rows), F32)
    parts = jnp.concatenate([*three_parts(x), filler], axis=0)
    turned = jnp.concatenate(
        [jnp.transpose(parts[:, head_at(a)]) for a in range(rows // LANES)], axis=0
    ).astype(BF16)
    line = lax.broadcasted_iota(jnp.int32, (LANES, heads * LANES), 0)
    lane = lax.broadcasted_iota(jnp.int32, (LANES, heads * LANES), 1)
    pick = (line < 3 * heads) & (lax.rem(line, heads) == lane // LANES)
    return jnp.dot(turned, jnp.where(pick, 1.0, 0.0).astype(BF16), preferred_element_type=F32)


def moved(*shapes):
    return sum(math.prod(s.shape) * jnp.dtype(s.dtype).itemsize for s in shapes)


def pack_kernel(order, me_ref, q_ref, k_ref, v_ref, *out_refs):
    for d, out_ref in zip(order, out_refs):
        lanes = pl.ds(pl.multiple_of(lax.bitwise_xor(me_ref[0], d) * LANES, LANES), LANES)
        for i, ref in enumerate((q_ref, k_ref, v_ref)):
            out_ref[i] = ref[:, lanes]


def pack(me, q, k, v, order, pieces=3):
    rows, width = q.shape
    piece = rows // pieces
    outs = [jax.ShapeDtypeStruct((3, rows, LANES), BF16)] * len(order)
    return pl.pallas_call(
        functools.partial(pack_kernel, order),
        grid_spec=pltpu.PrefetchScalarGridSpec(
            num_scalar_prefetch=1,
            grid=(pieces,),
            in_specs=[pl.BlockSpec((piece, width), lambda r, me: (r, 0))] * 3,
            out_specs=[pl.BlockSpec((3, piece, LANES), lambda r, me: (0, r, 0))] * len(order),
        ),
        out_shape=outs,
        cost_estimate=pl.CostEstimate(flops=0, bytes_accessed=2 * moved(*outs), transcendentals=0),
        name="pack",
    )(me, q, k, v)


def attend_kernel(order, rows, window, me_ref, *refs):
    came = refs[: len(order)]
    held_ref, o_ref, q_ref, k_ref, v_ref, s_ref, p_ref, start_ref = refs[len(order) :]
    parts = len(order)
    per = rows // LANES
    factor = LANES ** (-0.5) * math.log2(math.e)
    i = pl.program_id(0)

    @pl.when(i == 0)
    def _():
        for d, ref in zip(order, came):
            at = pl.ds(pl.multiple_of(lax.bitwise_xor(me_ref[0], d) * rows, LANES), rows)
            q_ref[at, :] = ref[0]
            k_ref[at, :] = ref[1]
            v_ref[at, :LANES] = ref[2]
        v_ref[:, LANES:] = jnp.ones((parts * rows, LANES), BF16)
        docs = held_ref[:, LANES : LANES + META, :].astype(F32)
        line = lax.broadcasted_iota(jnp.int32, docs.shape, 1)
        used = (line >= DOC_LINE) & (line < DOC_LINE + per)
        for d in range(LAST_DOC_ID):
            start_ref[d] = jnp.sum(jnp.where(used & (docs < d + 1), 1.0, 0.0)).astype(jnp.int32)

    wide = (TILE, LANES)
    lane = lax.broadcasted_iota(jnp.int32, wide, 1)
    sub = lax.broadcasted_iota(jnp.int32, wide, 0)
    first = pl.multiple_of(i * TILE, TILE)
    low, high = 0, 0
    for d in range(LAST_DOC_ID):
        low = jnp.where(first >= start_ref[d], start_ref[d], low)
        high = jnp.where(first + TILE - 1 >= start_ref[d], start_ref[d], high)
    count = i - low // TILE + 1

    def run(n, mixed):
        base = pl.multiple_of((i - (n - 1)) * TILE, TILE)
        keys = pl.ds(base, n * TILE)
        queries = q_ref[pl.ds(first, TILE), :]
        if mixed:
            begin = jnp.zeros(wide, jnp.int32)
            for d in range(LAST_DOC_ID):
                begin = jnp.where(sub >= start_ref[d] - first, start_ref[d], begin)
            begin = begin - lane
        else:
            begin = low - lane
        top = jnp.full(wide, MASKED, F32)
        scores = nt_dot(queries, k_ref[keys, :])
        for c in range(n * TILE // LANES):
            at = head_at(c)
            piece = scores[:, at]
            if mixed or c < TILE // LANES:
                piece = jnp.where(begin <= base + c * LANES, piece, MASKED)
            ahead = c * LANES - (n - 1) * TILE
            if ahead >= 0:
                piece = jnp.where(lane - sub <= -ahead, piece, MASKED)
            top = jnp.maximum(top, piece)
            s_ref[:, at] = piece
        row_max = jnp.max(top, axis=1, keepdims=True) * factor
        for c in range(n * TILE // LANES):
            at = head_at(c)
            p_ref[:, at] = jnp.exp2(s_ref[:, at] * factor - row_max).astype(BF16)
        total = jnp.dot(p_ref[:, : n * TILE], v_ref[keys, :], preferred_element_type=F32)
        o_ref[...] = (total[:, :LANES] / total[:, LANES:]).astype(BF16)

    for n in range(1, window + 1):
        pl.when((count == n) & (low == high))(functools.partial(run, n, False))
        pl.when((count == n) & (low != high))(functools.partial(run, n, True))


def attend(me, came, held, order, longest):
    rows = came[0].shape[1]
    tokens = len(order) * rows
    window = min((longest - 1 + TILE - 1) // TILE + 1, tokens // TILE)
    out = jax.ShapeDtypeStruct((tokens, LANES), BF16)
    return pl.pallas_call(
        functools.partial(attend_kernel, order, rows, window),
        grid=(tokens // TILE,),
        in_specs=[pl.BlockSpec(memory_space=pltpu.SMEM)] + [IN_VMEM] * (len(order) + 1),
        out_specs=pl.BlockSpec((TILE, LANES), lambda i: (i, 0)),
        out_shape=out,
        scratch_shapes=[
            pltpu.VMEM((tokens, LANES), BF16),
            pltpu.VMEM((tokens, LANES), BF16),
            pltpu.VMEM((tokens, 2 * LANES), BF16),
            pltpu.VMEM((TILE, window * TILE), F32),
            pltpu.VMEM((TILE, window * TILE), BF16),
            pltpu.SMEM((LAST_DOC_ID,), jnp.int32),
        ],
        cost_estimate=pl.CostEstimate(
            flops=2 * tokens * longest * LANES * 2,
            bytes_accessed=moved(*came, held, out),
            transcendentals=tokens * longest // 2,
        ),
        compiler_params=PARAMS,
        name="attend",
    )(me, *came, held)


def attend_gathered(q, k, v, doc_ids, heads):
    rows = q.shape[0]
    keys = lax.all_gather(k, "ctx", axis=0, tiled=True)
    values = lax.all_gather(v, "ctx", axis=0, tiled=True)
    docs = lax.all_gather(doc_ids, "ctx", axis=0, tiled=True)
    position = lax.axis_index("ctx") * rows + jnp.arange(rows)
    allowed = (jnp.arange(docs.shape[0])[None, :] <= position[:, None]) & (
        docs[None, :] == doc_ids[:, None]
    )

    def one(h):
        queries, head_keys, head_values = (
            lax.dynamic_slice_in_dim(a, h * LANES, LANES, 1) for a in (q, keys, values)
        )
        scores = jnp.where(allowed, nt_dot(queries, head_keys) * LANES ** (-0.5), MASKED)
        weights = jnp.exp(scores - jnp.max(scores, axis=1, keepdims=True))
        mixed = jnp.dot(weights.astype(BF16), head_values, preferred_element_type=F32)
        return (mixed / jnp.sum(weights, axis=1, keepdims=True)).astype(BF16)

    return lax.map(one, jnp.arange(heads)).transpose(1, 0, 2).reshape(rows, heads * LANES)


def local_state_kernel(gate_ref, doc_ref, k_ref, v_ref, out_ref, cum_ref):
    heads, rows = gate_ref.shape
    cumulated = cumulate(gate_ref[...])
    cum_ref[...] = cumulated
    last = cumulated[:, rows - 1 : rows]
    doc = doc_ref[...]
    start, end = doc[:, 0:1], doc[:, rows - 1 : rows]
    weight = jnp.where(doc == end, jnp.exp(last - cumulated), 0.0)
    through = jnp.exp(last) * jnp.where(start == end, 1.0, 0.0)
    line = lax.broadcasted_iota(jnp.int32, (META, LANES), 0)
    common = jnp.where(line == 2, start.astype(F32), jnp.where(line == 3, end.astype(F32), 0.0))
    for a in range(rows // LANES):
        common = jnp.where(line == DOC_LINE + a, doc[:, head_at(a)].astype(F32), common)
    for h in range(heads):
        at = head_at(h)
        turned = jnp.transpose(k_ref[:, at]).astype(F32)
        weighted = (turned * weight[h : h + 1, :]).astype(BF16)
        out_ref[h, :LANES] = jnp.dot(weighted, v_ref[:, at], preferred_element_type=F32).astype(BF16)
        whole = through[h : h + 1, :]
        high = whole.astype(BF16).astype(F32)
        meta = jnp.where(line == 0, high, jnp.where(line == 1, whole - high, common))
        out_ref[h, LANES:] = meta.astype(BF16)


def local_state(k, v, gates, doc_row):
    heads, rows = gates.shape
    outs = [
        jax.ShapeDtypeStruct((heads, LANES + META, LANES), BF16),
        jax.ShapeDtypeStruct((heads, rows), F32),
    ]
    return pl.pallas_call(
        local_state_kernel,
        in_specs=[IN_VMEM] * 4,
        out_specs=[IN_VMEM] * 2,
        out_shape=outs,
        cost_estimate=pl.CostEstimate(
            flops=2 * heads * rows * LANES * LANES,
            bytes_accessed=moved(k, v, gates, *outs),
            transcendentals=heads * rows,
        ),
        compiler_params=PARAMS,
        name="local_state",
    )(gates, doc_row, k, v)


def carry_kernel(held_ref, out_ref):
    parts = held_ref.shape[0]
    line = lax.broadcasted_iota(jnp.int32, (META, LANES), 0)
    state = jnp.zeros((LANES, LANES), F32)
    before = jnp.full((1, LANES), -1.0, F32)
    for j in range(parts):
        out_ref[j, :LANES] = state.astype(BF16)
        out_ref[j, LANES:] = jnp.where(line == 3, before, 0.0).astype(BF16)
        meta = held_ref[j, LANES:].astype(F32)
        through = jnp.where(meta[2:3] == before, meta[0:1] + meta[1:2], 0.0)
        state = state * through + held_ref[j, :LANES].astype(F32)
        before = meta[3:4]


def carry(held):
    return pl.pallas_call(
        carry_kernel,
        in_specs=[IN_VMEM],
        out_specs=IN_VMEM,
        out_shape=jax.ShapeDtypeStruct(held.shape, BF16),
        cost_estimate=pl.CostEstimate(
            flops=2 * held.size, bytes_accessed=2 * moved(held), transcendentals=0
        ),
        name="carry",
    )(held)


def carry_gathered(block):
    every = lax.all_gather(block, "ctx")
    state = jnp.zeros(block[:, :LANES].shape, F32)
    before = jnp.full((LANES,), -1.0, F32)

    def one(j, carried):
        state, before = carried
        here = lax.dynamic_index_in_dim(every, j, 0, False).astype(F32)
        meta = here[:, LANES:]
        through = jnp.where(meta[:, 2] == before, meta[:, 0] + meta[:, 1], 0.0)
        return state * through[:, None, :] + here[:, :LANES], meta[0, 3]

    state, before = lax.fori_loop(0, lax.axis_index("ctx"), one, (state, before))
    tail = jnp.zeros((block.shape[0], META, LANES), F32).at[:, 3].set(before)
    return jnp.concatenate([state, tail], axis=1).astype(BF16)


def inside_kernel(cum_ref, doc_ref, q_ref, k_ref, v_ref, raw_ref, column_ref, bias_ref):
    heads, rows = cum_ref.shape
    count = rows // LANES
    column_ref[...] = columns(cum_ref[...])
    doc = doc_ref[...].astype(F32)
    square = (LANES, LANES)
    upto = lax.broadcasted_iota(jnp.int32, square, 0) >= lax.broadcasted_iota(jnp.int32, square, 1)
    for a in range(count):
        doc_column = column_of(doc[:, head_at(a)])
        for b in range(a + 1):
            ok = doc_column == doc[:, head_at(b)]
            ok = ok & upto if a == b else ok
            bias_ref[head_at(a), head_at(b)] = jnp.where(ok, 0.0, MASKED)
    for h in range(heads):
        at = head_at(h)
        row = cum_ref[h : h + 1, :]
        for a in range(count):
            lines = head_at(a)
            width = (a + 1) * LANES
            scores = nt_dot(q_ref[lines, at], k_ref[0:width, at])
            spread = jnp.concatenate([column_ref[lines, at]] * (a + 1), axis=1) - row[:, :width]
            decayed = scores * jnp.exp(spread + bias_ref[lines, 0:width])
            raw_ref[lines, at] = jnp.dot(
                decayed.astype(BF16), v_ref[0:width, at], preferred_element_type=F32
            )


def inside(q, k, v, cumulated, doc_row):
    heads, rows = cumulated.shape
    out = jax.ShapeDtypeStruct(q.shape, F32)
    return pl.pallas_call(
        inside_kernel,
        in_specs=[IN_VMEM] * 5,
        out_specs=IN_VMEM,
        out_shape=out,
        scratch_shapes=[pltpu.VMEM(q.shape, F32), pltpu.VMEM((rows, rows), F32)],
        cost_estimate=pl.CostEstimate(
            flops=3 * heads * rows * rows * LANES,
            bytes_accessed=moved(q, k, v, out),
            transcendentals=heads * rows * rows // 2,
        ),
        compiler_params=PARAMS,
        name="inside",
    )(cumulated, doc_row, q, k, v)


def incoming_kernel(cum_ref, doc_ref, q_ref, before_ref, raw_ref, out_ref, square_ref):
    heads, rows = cum_ref.shape
    factor = columns(jnp.exp(cum_ref[...]))
    doc = doc_ref[...].astype(F32)
    meta = before_ref[0, LANES:].astype(F32)
    linked = jnp.concatenate(
        [jnp.where(column_of(doc[:, head_at(a)]) == meta[3:4], 1.0, 0.0) for a in range(rows // LANES)],
        axis=0,
    )
    total = jnp.zeros((rows, LANES), F32)
    for h in range(heads):
        at = head_at(h)
        came = jnp.dot(q_ref[:, at], before_ref[h, :LANES], preferred_element_type=F32)
        raw = raw_ref[:, at] + came * (factor[:, at] * linked)
        out_ref[:, at] = raw
        total = total + raw * raw
    square_ref[...] = nt_dot(jnp.ones((8, LANES), F32), total, HIGHEST)


def incoming(q, cumulated, doc_row, before, raw):
    heads, rows = cumulated.shape
    outs = [jax.ShapeDtypeStruct(q.shape, F32), jax.ShapeDtypeStruct((8, rows), F32)]
    return pl.pallas_call(
        incoming_kernel,
        in_specs=[IN_VMEM] * 5,
        out_specs=[IN_VMEM] * 2,
        out_shape=outs,
        cost_estimate=pl.CostEstimate(
            flops=2 * heads * rows * LANES * LANES,
            bytes_accessed=moved(q, before, raw, *outs),
            transcendentals=heads * rows,
        ),
        compiler_params=PARAMS,
        name="incoming",
    )(cumulated, doc_row, q, before, raw)


def normalize_kernel(features, raw_ref, gain_ref, *refs):
    *squares, out_ref = refs
    total = squares[0][...]
    for ref in squares[1:]:
        total = total + ref[...]
    scale = column_of(lax.rsqrt(total / features + EPSILON)[0:1])
    for h in range(raw_ref.shape[1] // LANES):
        at = head_at(h)
        out_ref[:, at] = (raw_ref[:, at] * scale * gain_ref[:, at]).astype(BF16)


def normalize(raw, gain_row, squares, features):
    rows, width = raw.shape
    line = pl.BlockSpec((LANES, width), lambda r: (r, 0))
    out = jax.ShapeDtypeStruct((rows, width), BF16)
    return pl.pallas_call(
        functools.partial(normalize_kernel, features),
        grid=(rows // LANES,),
        in_specs=[line, pl.BlockSpec((1, width), lambda r: (0, 0))]
        + [pl.BlockSpec((8, LANES), lambda r: (0, r))] * len(squares),
        out_specs=line,
        out_shape=out,
        cost_estimate=pl.CostEstimate(
            flops=3 * raw.size, bytes_accessed=moved(raw, out), transcendentals=rows
        ),
        name="normalize",
    )(raw, gain_row, *squares)


def after(x, *earlier):
    return lax.optimization_barrier((x, *earlier))[0]


def exchange(x):
    return lax.all_to_all(x, "ctx", split_axis=0, concat_axis=0, tiled=True)


def on_device(size, head_parts, q_lin, k_lin, v_lin, gate_log, lin_gain, q_soft, k_soft, v_soft, doc_ids):
    heads, rows = gate_log.shape
    doc_row = doc_ids.reshape(1, rows)

    if heads == size and size & (size - 1) == 0:
        me = lax.axis_index("ctx").reshape(1)

        def swap(x, d):
            return lax.ppermute(x, "ctx", [(i, i ^ d) for i in range(size)])

        order = [d for d in range(size - 2, 0, -2)] + [d for d in range(size - 1, 0, -2)] + [0]
        early = size // 2 - 1
        sent = pack(me, q_soft, k_soft, v_soft, order)
        came = [swap(sent[i], order[i]) for i in range(early)]
        states, cumulated = local_state(after(k_lin, sent[-1]), v_lin, gate_log, doc_row)
        held_states = exchange(states)
        late, _ = lax.optimization_barrier((sent[early:-1], states))
        came += [swap(x, d) for x, d in zip(late, order[early:])]
        passed = carry(held_states)
        before = exchange(passed)
        raw = inside(after(q_lin, passed), k_lin, v_lin, cumulated, doc_row)
        mixed = attend(me, [*came, after(sent[-1], raw)], held_states, order, rows * size // 2)
        back = exchange(mixed.reshape(size, rows, LANES))
        raw, square = incoming(q_lin, cumulated, doc_row, after(before, mixed), raw)
        soft_out = back.transpose(1, 0, 2).reshape(rows, heads * LANES)
    else:
        states, cumulated = local_state(k_lin, v_lin, gate_log, doc_row)
        raw = inside(q_lin, k_lin, v_lin, cumulated, doc_row)
        raw, square = incoming(q_lin, cumulated, doc_row, carry_gathered(states), raw)
        soft_out = attend_gathered(q_soft, k_soft, v_soft, doc_ids, heads)

    squares = [square]
    for d in range(1, head_parts):
        turn = [(i, (i + d) % head_parts) for i in range(head_parts)]
        squares.append(lax.ppermute(square, "head", turn))
    lin_out = normalize(raw, lin_gain.reshape(1, -1), squares, heads * head_parts * LANES)
    return lin_out, soft_out


def solution(mesh):
    split = P("ctx", "head")
    in_specs = (split, split, split, P("head", "ctx"), P("head"), split, split, split, P("ctx"))
    return jax.shard_map(
        functools.partial(on_device, mesh.shape["ctx"], mesh.shape["head"]),
        mesh=mesh,
        in_specs=in_specs,
        out_specs=(split, split),
        check_vma=False,
    )
```

```python
import functools
import math

import jax
import jax.numpy as jnp
from jax import lax
from jax.experimental import pallas as pl
from jax.experimental.pallas import tpu as pltpu
from jax.sharding import PartitionSpec as P

EPSILON = 1e-05
MASKED = -1e30
LANES = 128
META = 16
DOC_LINE = 4
LAST_DOC_ID = 7
TILE = 256
CHAINS = 2
F32 = jnp.float32
BF16 = jnp.bfloat16
HIGHEST = lax.Precision.HIGHEST
IN_VMEM = pl.BlockSpec(memory_space=pltpu.VMEM)
IN_HBM = pl.BlockSpec(memory_space=pltpu.HBM)
PARAMS = pltpu.CompilerParams(vmem_limit_bytes=48 << 20)


def nt_dot(a, b, precision=None):
    return lax.dot_general(
        a, b, (((1,), (1,)), ((), ())), precision=precision, preferred_element_type=F32
    )


def head_at(h):
    return slice(h * LANES, (h + 1) * LANES)


def column_of(row):
    return jnp.transpose(jnp.broadcast_to(row, (LANES, LANES)))


def three_parts(x):
    a = x.astype(BF16).astype(F32)
    b = (x - a).astype(BF16).astype(F32)
    return a, b, x - a - b


def cumulate(gates):
    heads, rows = gates.shape
    lower = lax.broadcasted_iota(jnp.int32, (rows, rows), 0) <= lax.broadcasted_iota(
        jnp.int32, (rows, rows), 1
    )
    parts = jnp.concatenate([*three_parts(gates), jnp.zeros_like(gates)], axis=0).astype(BF16)
    sums = jnp.dot(parts, jnp.where(lower, 1.0, 0.0).astype(BF16), preferred_element_type=F32)
    return sums[:heads] + sums[heads : 2 * heads] + sums[2 * heads : 3 * heads]


def columns(x):
    heads, rows = x.shape
    filler = jnp.zeros((LANES - 3 * heads, rows), F32)
    parts = jnp.concatenate([*three_parts(x), filler], axis=0)
    turned = jnp.concatenate(
        [jnp.transpose(parts[:, head_at(a)]) for a in range(rows // LANES)], axis=0
    ).astype(BF16)
    line = lax.broadcasted_iota(jnp.int32, (LANES, heads * LANES), 0)
    lane = lax.broadcasted_iota(jnp.int32, (LANES, heads * LANES), 1)
    pick = (line < 3 * heads) & (lax.rem(line, heads) == lane // LANES)
    return jnp.dot(turned, jnp.where(pick, 1.0, 0.0).astype(BF16), preferred_element_type=F32)


def moved(*shapes):
    return sum(math.prod(s.shape) * jnp.dtype(s.dtype).itemsize for s in shapes)


def pack_kernel(order, me_ref, *refs):
    ins, outs, (held_ref, in_sems, out_sems) = refs[:3], refs[3:-3], refs[-3:]
    coming, going = [], []
    for n, d in enumerate(order):
        lanes = pl.ds(pl.multiple_of(lax.bitwise_xor(me_ref[0], d) * LANES, LANES), LANES)
        for i, ref in enumerate(ins):
            coming.append(
                pltpu.make_async_copy(ref.at[:, lanes], held_ref.at[n, i], in_sems.at[3 * n + i])
            )
            coming[-1].start()
    for n, out_ref in enumerate(outs):
        for copy in coming[3 * n : 3 * n + 3]:
            copy.wait()
        going.append(pltpu.make_async_copy(held_ref.at[n], out_ref, out_sems.at[n]))
        going[-1].start()
    for copy in going:
        copy.wait()


def pack(me, q, k, v, order):
    rows = q.shape[0]
    n = len(order)
    outs = [jax.ShapeDtypeStruct((3, rows, LANES), BF16)] * n
    return pl.pallas_call(
        functools.partial(pack_kernel, order),
        in_specs=[pl.BlockSpec(memory_space=pltpu.SMEM)] + [IN_HBM] * 3,
        out_specs=[IN_HBM] * n,
        out_shape=outs,
        scratch_shapes=[
            pltpu.VMEM((n, 3, rows, LANES), BF16),
            pltpu.SemaphoreType.DMA((3 * n,)),
            pltpu.SemaphoreType.DMA((n,)),
        ],
        cost_estimate=pl.CostEstimate(flops=0, bytes_accessed=2 * moved(*outs), transcendentals=0),
        name="pack",
    )(me, q, k, v)


def attend_kernel(order, rows, window, me_ref, *refs):
    came = refs[: len(order)]
    held_ref, out_ref, q_ref, k_ref, v_ref, meta_ref, o_ref, s_ref, in_sems, out_sems = refs[
        len(order) :
    ]
    parts = len(order)
    per = rows // LANES
    factor = LANES ** (-0.5) * math.log2(math.e)
    meta_copy = pltpu.make_async_copy(
        held_ref.at[:, pl.ds(LANES, META), :], meta_ref, in_sems.at[3 * parts]
    )
    meta_copy.start()
    copies = []
    for n, (d, ref) in enumerate(zip(order, came)):
        at = pl.ds(pl.multiple_of(lax.bitwise_xor(me_ref[0], d) * rows, LANES), rows)
        for j, target in enumerate((q_ref.at[at], k_ref.at[at], v_ref.at[at, pl.ds(0, LANES)])):
            copies.append(pltpu.make_async_copy(ref.at[j], target, in_sems.at[3 * n + j]))
            copies[-1].start()
    v_ref[:, LANES:] = jnp.ones((parts * rows, LANES), BF16)
    meta_copy.wait()
    docs = meta_ref[...].astype(F32)
    line = lax.broadcasted_iota(jnp.int32, docs.shape, 1)
    used = (line >= DOC_LINE) & (line < DOC_LINE + per)
    starts = [
        jnp.sum(jnp.where(used & (docs < d), 1.0, 0.0)).astype(jnp.int32)
        for d in range(1, LAST_DOC_ID + 1)
    ]
    for copy in copies:
        copy.wait()

    wide = (TILE, LANES)
    lane = lax.broadcasted_iota(jnp.int32, wide, 1)
    sub = lax.broadcasted_iota(jnp.int32, wide, 0)
    step = CHAINS * TILE

    def body(i, carry):
        first = pl.multiple_of(i * step, step)
        low = 0
        for s in starts:
            low = jnp.where(first >= s, s, low)
        count = (i + 1) * CHAINS - low // TILE

        def run(n):
            base = pl.multiple_of(first + step - n * TILE, TILE)
            tops = {}

            def score(chain):
                tiles = n - CHAINS + 1 + chain
                mine = pl.multiple_of(first + chain * TILE, TILE)
                keys = pl.ds(base, tiles * TILE)
                begin = jnp.zeros(wide, jnp.int32)
                for s in starts:
                    begin = jnp.where(sub >= s - mine, s, begin)
                begin = begin - base - lane
                top = jnp.full(wide, MASKED, F32)
                queries = q_ref[pl.ds(mine, TILE), :]
                for c in range(tiles * TILE // LANES):
                    at = head_at(c)
                    if c % 2 == 0:
                        scores = nt_dot(queries, k_ref[pl.ds(pl.multiple_of(base + c * LANES, LANES), 2 * LANES), :])
                    piece = jnp.where(begin <= c * LANES, scores[:, head_at(c % 2)], MASKED)
                    ahead = c * LANES - (tiles - 1) * TILE
                    if ahead >= 0:
                        piece = jnp.where(lane - sub <= -ahead, piece, MASKED)
                    top = jnp.maximum(top, piece)
                    s_ref[chain, :, at] = piece
                tops[chain] = jnp.max(top, axis=1, keepdims=True) * factor

            def mix(chain):
                tiles = n - CHAINS + 1 + chain
                mine = pl.multiple_of(first + chain * TILE, TILE)
                row_max = tops[chain]
                total = jnp.zeros((TILE, 2 * LANES), F32)
                for t in range(tiles):
                    at = slice(t * TILE, (t + 1) * TILE)
                    p = jnp.exp2(s_ref[chain, :, at] * factor - row_max).astype(BF16)
                    keys = pl.ds(pl.multiple_of(base + t * TILE, TILE), TILE)
                    total = total + jnp.dot(p, v_ref[keys, :], preferred_element_type=F32)
                o_ref[pl.ds(mine, TILE), :] = (total[:, :LANES] / total[:, LANES:]).astype(BF16)

            for chain in range(CHAINS):
                score(chain)
            for chain in range(CHAINS):
                mix(chain)

        for n in range(CHAINS, window + CHAINS):
            pl.when(count == n)(functools.partial(run, n))
        at = pl.ds(first, step)
        pltpu.make_async_copy(o_ref.at[at], out_ref.at[at], out_sems.at[i]).start()
        return carry

    blocks = parts * rows // step
    lax.fori_loop(0, blocks, body, 0)
    for i in range(blocks):
        at = pl.ds(i * step, step)
        pltpu.make_async_copy(o_ref.at[at], out_ref.at[at], out_sems.at[i]).wait()


def attend(me, came, held, order, longest):
    rows = came[0].shape[1]
    tokens = len(order) * rows
    window = min((longest - 1 + TILE - 1) // TILE + 1, tokens // TILE - CHAINS + 1)
    out = jax.ShapeDtypeStruct((tokens, LANES), BF16)
    return pl.pallas_call(
        functools.partial(attend_kernel, order, rows, window),
        in_specs=[pl.BlockSpec(memory_space=pltpu.SMEM)] + [IN_HBM] * (len(order) + 1),
        out_specs=IN_HBM,
        out_shape=out,
        scratch_shapes=[
            pltpu.VMEM((tokens, LANES), BF16),
            pltpu.VMEM((tokens, LANES), BF16),
            pltpu.VMEM((tokens, 2 * LANES), BF16),
            pltpu.VMEM((len(order), META, LANES), BF16),
            pltpu.VMEM((tokens, LANES), BF16),
            pltpu.VMEM((CHAINS, TILE, (window + CHAINS - 1) * TILE), F32),
            pltpu.SemaphoreType.DMA((3 * len(order) + 1,)),
            pltpu.SemaphoreType.DMA((tokens // (CHAINS * TILE),)),
        ],
        cost_estimate=pl.CostEstimate(
            flops=2 * tokens * longest * LANES * 2,
            bytes_accessed=moved(*came, held, out),
            transcendentals=tokens * longest // 2,
        ),
        compiler_params=PARAMS,
        name="attend",
    )(me, *came, held)


def attend_gathered(q, k, v, doc_ids, heads):
    rows = q.shape[0]
    keys = lax.all_gather(k, "ctx", axis=0, tiled=True)
    values = lax.all_gather(v, "ctx", axis=0, tiled=True)
    docs = lax.all_gather(doc_ids, "ctx", axis=0, tiled=True)
    position = lax.axis_index("ctx") * rows + jnp.arange(rows)
    allowed = (jnp.arange(docs.shape[0])[None, :] <= position[:, None]) & (
        docs[None, :] == doc_ids[:, None]
    )

    def one(h):
        queries, head_keys, head_values = (
            lax.dynamic_slice_in_dim(a, h * LANES, LANES, 1) for a in (q, keys, values)
        )
        scores = jnp.where(allowed, nt_dot(queries, head_keys) * LANES ** (-0.5), MASKED)
        weights = jnp.exp(scores - jnp.max(scores, axis=1, keepdims=True))
        mixed = jnp.dot(weights.astype(BF16), head_values, preferred_element_type=F32)
        return (mixed / jnp.sum(weights, axis=1, keepdims=True)).astype(BF16)

    return lax.map(one, jnp.arange(heads)).transpose(1, 0, 2).reshape(rows, heads * LANES)


def local_state_kernel(gate_ref, doc_ref, k_ref, v_ref, out_ref, cum_ref):
    heads, rows = gate_ref.shape
    cumulated = cumulate(gate_ref[...])
    cum_ref[...] = cumulated
    last = cumulated[:, rows - 1 : rows]
    doc = doc_ref[...]
    start, end = doc[:, 0:1], doc[:, rows - 1 : rows]
    weight = jnp.where(doc == end, jnp.exp(last - cumulated), 0.0)
    through = jnp.exp(last) * jnp.where(start == end, 1.0, 0.0)
    line = lax.broadcasted_iota(jnp.int32, (META, LANES), 0)
    common = jnp.where(line == 2, start.astype(F32), jnp.where(line == 3, end.astype(F32), 0.0))
    for a in range(rows // LANES):
        common = jnp.where(line == DOC_LINE + a, doc[:, head_at(a)].astype(F32), common)
    for h in range(heads):
        at = head_at(h)
        turned = jnp.transpose(k_ref[:, at]).astype(F32)
        weighted = (turned * weight[h : h + 1, :]).astype(BF16)
        out_ref[h, :LANES] = jnp.dot(weighted, v_ref[:, at], preferred_element_type=F32).astype(BF16)
        whole = through[h : h + 1, :]
        high = whole.astype(BF16).astype(F32)
        meta = jnp.where(line == 0, high, jnp.where(line == 1, whole - high, common))
        out_ref[h, LANES:] = meta.astype(BF16)


def local_state(k, v, gates, doc_row):
    heads, rows = gates.shape
    outs = [
        jax.ShapeDtypeStruct((heads, LANES + META, LANES), BF16),
        jax.ShapeDtypeStruct((heads, rows), F32),
    ]
    return pl.pallas_call(
        local_state_kernel,
        in_specs=[IN_VMEM] * 4,
        out_specs=[IN_VMEM] * 2,
        out_shape=outs,
        cost_estimate=pl.CostEstimate(
            flops=2 * heads * rows * LANES * LANES,
            bytes_accessed=moved(k, v, gates, *outs),
            transcendentals=heads * rows,
        ),
        compiler_params=PARAMS,
        name="local_state",
    )(gates, doc_row, k, v)


def carry_kernel(came_ref, out_ref, held_ref, sems):
    parts = came_ref.shape[0]
    copies = [pltpu.make_async_copy(came_ref.at[j], held_ref.at[j], sems.at[j]) for j in range(parts)]
    for copy in copies:
        copy.start()
    line = lax.broadcasted_iota(jnp.int32, (META, LANES), 0)
    state = jnp.zeros((LANES, LANES), F32)
    before = jnp.full((1, LANES), -1.0, F32)
    for j in range(parts):
        out_ref[j, :LANES] = state.astype(BF16)
        out_ref[j, LANES:] = jnp.where(line == 3, before, 0.0).astype(BF16)
        copies[j].wait()
        meta = held_ref[j, LANES:].astype(F32)
        through = jnp.where(meta[2:3] == before, meta[0:1] + meta[1:2], 0.0)
        state = state * through + held_ref[j, :LANES].astype(F32)
        before = meta[3:4]


def carry(came):
    return pl.pallas_call(
        carry_kernel,
        in_specs=[IN_HBM],
        out_specs=IN_VMEM,
        out_shape=jax.ShapeDtypeStruct(came.shape, BF16),
        scratch_shapes=[pltpu.VMEM(came.shape, BF16), pltpu.SemaphoreType.DMA((came.shape[0],))],
        cost_estimate=pl.CostEstimate(
            flops=2 * came.size, bytes_accessed=2 * moved(came), transcendentals=0
        ),
        name="carry",
    )(came)


def carry_gathered(block):
    every = lax.all_gather(block, "ctx")
    state = jnp.zeros(block[:, :LANES].shape, F32)
    before = jnp.full((LANES,), -1.0, F32)

    def one(j, carried):
        state, before = carried
        here = lax.dynamic_index_in_dim(every, j, 0, False).astype(F32)
        meta = here[:, LANES:]
        through = jnp.where(meta[:, 2] == before, meta[:, 0] + meta[:, 1], 0.0)
        return state * through[:, None, :] + here[:, :LANES], meta[0, 3]

    state, before = lax.fori_loop(0, lax.axis_index("ctx"), one, (state, before))
    tail = jnp.zeros((block.shape[0], META, LANES), F32).at[:, 3].set(before)
    return jnp.concatenate([state, tail], axis=1).astype(BF16)


def inside_kernel(cum_ref, doc_ref, q_hbm, k_ref, v_ref, raw_ref, q_ref, sem, column_ref, bias_ref):
    copy = pltpu.make_async_copy(q_hbm, q_ref, sem)
    copy.start()
    heads, rows = cum_ref.shape
    count = rows // LANES
    column_ref[...] = columns(cum_ref[...])
    doc = doc_ref[...].astype(F32)
    square = (LANES, LANES)
    upto = lax.broadcasted_iota(jnp.int32, square, 0) >= lax.broadcasted_iota(jnp.int32, square, 1)
    for a in range(count):
        doc_column = column_of(doc[:, head_at(a)])
        for b in range(a + 1):
            ok = doc_column == doc[:, head_at(b)]
            ok = ok & upto if a == b else ok
            bias_ref[head_at(a), head_at(b)] = jnp.where(ok, 0.0, MASKED)
    copy.wait()
    for h in range(heads):
        at = head_at(h)
        row = cum_ref[h : h + 1, :]
        for a in range(count):
            lines = head_at(a)
            width = (a + 1) * LANES
            scores = nt_dot(q_ref[lines, at], k_ref[0:width, at])
            spread = jnp.concatenate([column_ref[lines, at]] * (a + 1), axis=1) - row[:, :width]
            decayed = scores * jnp.exp(spread + bias_ref[lines, 0:width])
            raw_ref[lines, at] = jnp.dot(
                decayed.astype(BF16), v_ref[0:width, at], preferred_element_type=F32
            )


def inside(q, k, v, cumulated, doc_row):
    heads, rows = cumulated.shape
    out = jax.ShapeDtypeStruct(q.shape, F32)
    return pl.pallas_call(
        inside_kernel,
        in_specs=[IN_VMEM, IN_VMEM, IN_HBM, IN_VMEM, IN_VMEM],
        out_specs=IN_VMEM,
        out_shape=out,
        scratch_shapes=[
            pltpu.VMEM(q.shape, BF16),
            pltpu.SemaphoreType.DMA,
            pltpu.VMEM(q.shape, F32),
            pltpu.VMEM((rows, rows), F32),
        ],
        cost_estimate=pl.CostEstimate(
            flops=3 * heads * rows * rows * LANES,
            bytes_accessed=moved(q, k, v, out),
            transcendentals=heads * rows * rows // 2,
        ),
        compiler_params=PARAMS,
        name="inside",
    )(cumulated, doc_row, q, k, v)


def incoming_kernel(cum_ref, doc_ref, q_hbm, before_ref, raw_ref, out_ref, square_ref, q_ref, sem):
    copy = pltpu.make_async_copy(q_hbm, q_ref, sem)
    copy.start()
    heads, rows = cum_ref.shape
    factor = columns(jnp.exp(cum_ref[...]))
    doc = doc_ref[...].astype(F32)
    meta = before_ref[0, LANES:].astype(F32)
    linked = jnp.concatenate(
        [jnp.where(column_of(doc[:, head_at(a)]) == meta[3:4], 1.0, 0.0) for a in range(rows // LANES)],
        axis=0,
    )
    total = jnp.zeros((rows, LANES), F32)
    copy.wait()
    for h in range(heads):
        at = head_at(h)
        came = jnp.dot(q_ref[:, at], before_ref[h, :LANES], preferred_element_type=F32)
        raw = raw_ref[:, at] + came * (factor[:, at] * linked)
        out_ref[:, at] = raw
        total = total + raw * raw
    square_ref[...] = nt_dot(jnp.ones((8, LANES), F32), total, HIGHEST)


def incoming(q, cumulated, doc_row, before, raw):
    heads, rows = cumulated.shape
    outs = [jax.ShapeDtypeStruct(q.shape, F32), jax.ShapeDtypeStruct((8, rows), F32)]
    return pl.pallas_call(
        incoming_kernel,
        in_specs=[IN_VMEM, IN_VMEM, IN_HBM, IN_VMEM, IN_VMEM],
        out_specs=[IN_VMEM] * 2,
        out_shape=outs,
        scratch_shapes=[pltpu.VMEM(q.shape, BF16), pltpu.SemaphoreType.DMA],
        cost_estimate=pl.CostEstimate(
            flops=2 * heads * rows * LANES * LANES,
            bytes_accessed=moved(q, before, raw, *outs),
            transcendentals=heads * rows,
        ),
        compiler_params=PARAMS,
        name="incoming",
    )(cumulated, doc_row, q, before, raw)


def normalize_kernel(features, raw_ref, gain_ref, *refs):
    *squares, out_ref, made_ref, sems = refs
    total = squares[0][...]
    for ref in squares[1:]:
        total = total + ref[...]
    scale = lax.rsqrt(total / features + EPSILON)
    copies = []
    for a in range(raw_ref.shape[0] // LANES):
        lines = head_at(a)
        column = column_of(scale[0:1, lines])
        for h in range(raw_ref.shape[1] // LANES):
            at = head_at(h)
            made_ref[lines, at] = (raw_ref[lines, at] * column * gain_ref[:, at]).astype(BF16)
        copies.append(pltpu.make_async_copy(made_ref.at[lines], out_ref.at[lines], sems.at[a]))
        copies[-1].start()
    for copy in copies:
        copy.wait()


def normalize(raw, gain_row, squares, features):
    rows, width = raw.shape
    out = jax.ShapeDtypeStruct((rows, width), BF16)
    return pl.pallas_call(
        functools.partial(normalize_kernel, features),
        in_specs=[IN_VMEM] * (2 + len(squares)),
        out_specs=IN_HBM,
        out_shape=out,
        scratch_shapes=[
            pltpu.VMEM((rows, width), BF16),
            pltpu.SemaphoreType.DMA((rows // LANES,)),
        ],
        cost_estimate=pl.CostEstimate(
            flops=3 * raw.size, bytes_accessed=moved(raw, out), transcendentals=rows
        ),
        compiler_params=PARAMS,
        name="normalize",
    )(raw, gain_row, *squares)


def after(x, *earlier):
    return lax.optimization_barrier((x, *earlier))[0]


def exchange(x):
    return lax.all_to_all(x, "ctx", split_axis=0, concat_axis=0, tiled=True)


def on_device(size, head_parts, q_lin, k_lin, v_lin, gate_log, lin_gain, q_soft, k_soft, v_soft, doc_ids):
    heads, rows = gate_log.shape
    doc_row = doc_ids.reshape(1, rows)

    if heads == size and size & (size - 1) == 0:
        me = lax.axis_index("ctx").reshape(1)

        def swap(x, d):
            return lax.ppermute(x, "ctx", [(i, i ^ d) for i in range(size)])

        order = [d for d in range(size - 2, 0, -2)] + [d for d in range(size - 1, 0, -2)] + [0]
        first, second = size // 2 - 1, size // 2 + 1
        sent = pack(me, q_soft, k_soft, v_soft, order)
        came = [swap(x, d) for x, d in zip(sent[:first], order)]
        states, cumulated = local_state(after(k_lin, sent[-1]), v_lin, gate_log, doc_row)
        held_states = exchange(states)
        middle, _ = lax.optimization_barrier((sent[first:second], states))
        came += [swap(x, d) for x, d in zip(middle, order[first:])]
        raw = inside(after(q_lin, states), k_lin, v_lin, cumulated, doc_row)
        late, _, held_states = lax.optimization_barrier((sent[second:-1], raw, held_states))
        came += [swap(x, d) for x, d in zip(late, order[second:])]
        passed = carry(held_states)
        before = exchange(passed)
        mixed = attend(me, [*came, after(sent[-1], passed)], held_states, order, rows * size // 2)
        back = exchange(mixed.reshape(size, rows, LANES))
        raw, square = incoming(q_lin, cumulated, doc_row, after(before, mixed), raw)
        soft_out = back.transpose(1, 0, 2).reshape(rows, heads * LANES)
    else:
        states, cumulated = local_state(k_lin, v_lin, gate_log, doc_row)
        raw = inside(q_lin, k_lin, v_lin, cumulated, doc_row)
        raw, square = incoming(q_lin, cumulated, doc_row, carry_gathered(states), raw)
        soft_out = attend_gathered(q_soft, k_soft, v_soft, doc_ids, heads)

    squares = [square]
    for d in range(1, head_parts):
        turn = [(i, (i + d) % head_parts) for i in range(head_parts)]
        squares.append(lax.ppermute(square, "head", turn))
    lin_out = normalize(raw, lin_gain.reshape(1, -1), squares, heads * head_parts * LANES)
    return lin_out, soft_out


def solution(mesh):
    split = P("ctx", "head")
    in_specs = (split, split, split, P("head", "ctx"), P("head"), split, split, split, P("ctx"))
    return jax.shard_map(
        functools.partial(on_device, mesh.shape["ctx"], mesh.shape["head"]),
        mesh=mesh,
        in_specs=in_specs,
        out_specs=(split, split),
        check_vma=False,
    )
```

```python
import functools
import math

import jax
import jax.numpy as jnp
from jax import lax
from jax.experimental import pallas as pl
from jax.experimental.pallas import tpu as pltpu
from jax.sharding import PartitionSpec as P

EPSILON = 1e-05
MASKED = -1e30
LANES = 128
META = 16
DOC_LINE = 4
LAST_DOC_ID = 7
TILE = 256
CHAINS = 2
VMEM_MB = 16
F32 = jnp.float32
BF16 = jnp.bfloat16
HIGHEST = lax.Precision.HIGHEST
IN_VMEM = pl.BlockSpec(memory_space=pltpu.VMEM)
IN_HBM = pl.BlockSpec(memory_space=pltpu.HBM)
PARAMS = pltpu.CompilerParams(vmem_limit_bytes=VMEM_MB << 20)


def nt_dot(a, b, precision=None):
    return lax.dot_general(
        a, b, (((1,), (1,)), ((), ())), precision=precision, preferred_element_type=F32
    )


def head_at(h):
    return slice(h * LANES, (h + 1) * LANES)


def column_of(row):
    return jnp.transpose(jnp.broadcast_to(row, (LANES, LANES)))


def three_parts(x):
    a = x.astype(BF16).astype(F32)
    b = (x - a).astype(BF16).astype(F32)
    return a, b, x - a - b


def cumulate(gates):
    heads, rows = gates.shape
    lower = lax.broadcasted_iota(jnp.int32, (rows, rows), 0) <= lax.broadcasted_iota(
        jnp.int32, (rows, rows), 1
    )
    parts = jnp.concatenate([*three_parts(gates), jnp.zeros_like(gates)], axis=0).astype(BF16)
    sums = jnp.dot(parts, jnp.where(lower, 1.0, 0.0).astype(BF16), preferred_element_type=F32)
    return sums[:heads] + sums[heads : 2 * heads] + sums[2 * heads : 3 * heads]


def columns(x):
    heads, rows = x.shape
    filler = jnp.zeros((LANES - 3 * heads, rows), F32)
    parts = jnp.concatenate([*three_parts(x), filler], axis=0)
    turned = jnp.concatenate(
        [jnp.transpose(parts[:, head_at(a)]) for a in range(rows // LANES)], axis=0
    ).astype(BF16)
    line = lax.broadcasted_iota(jnp.int32, (LANES, heads * LANES), 0)
    lane = lax.broadcasted_iota(jnp.int32, (LANES, heads * LANES), 1)
    pick = (line < 3 * heads) & (lax.rem(line, heads) == lane // LANES)
    return jnp.dot(turned, jnp.where(pick, 1.0, 0.0).astype(BF16), preferred_element_type=F32)


def moved(*shapes):
    return sum(math.prod(s.shape) * jnp.dtype(s.dtype).itemsize for s in shapes)


def pack_kernel(order, me_ref, *refs):
    ins, outs, (held_ref, in_sems, out_sems) = refs[:3], refs[3:-3], refs[-3:]
    coming, going = [], []
    for n, d in enumerate(order):
        lanes = pl.ds(pl.multiple_of(lax.bitwise_xor(me_ref[0], d) * LANES, LANES), LANES)
        for i, ref in enumerate(ins):
            coming.append(
                pltpu.make_async_copy(ref.at[:, lanes], held_ref.at[n, i], in_sems.at[3 * n + i])
            )
            coming[-1].start()
    for n, out_ref in enumerate(outs):
        for copy in coming[3 * n : 3 * n + 3]:
            copy.wait()
        going.append(pltpu.make_async_copy(held_ref.at[n], out_ref, out_sems.at[n]))
        going[-1].start()
    for copy in going:
        copy.wait()


def pack(me, q, k, v, order):
    rows = q.shape[0]
    n = len(order)
    outs = [jax.ShapeDtypeStruct((3, rows, LANES), BF16)] * n
    return pl.pallas_call(
        functools.partial(pack_kernel, order),
        in_specs=[pl.BlockSpec(memory_space=pltpu.SMEM)] + [IN_HBM] * 3,
        out_specs=[IN_HBM] * n,
        out_shape=outs,
        scratch_shapes=[
            pltpu.VMEM((n, 3, rows, LANES), BF16),
            pltpu.SemaphoreType.DMA((3 * n,)),
            pltpu.SemaphoreType.DMA((n,)),
        ],
        cost_estimate=pl.CostEstimate(flops=0, bytes_accessed=2 * moved(*outs), transcendentals=0),
        name="pack",
    )(me, q, k, v)


def attend_kernel(order, rows, window, me_ref, *refs):
    came = refs[: len(order)]
    doc_ref, out_ref, q_ref, k_ref, v_ref, o_ref, s_ref, in_sems, out_sems = refs[len(order) :]
    parts = len(order)
    per = rows // LANES
    factor = LANES ** (-0.5) * math.log2(math.e)
    copies = []
    for n, (d, ref) in enumerate(zip(order, came)):
        at = pl.ds(pl.multiple_of(lax.bitwise_xor(me_ref[0], d) * rows, LANES), rows)
        for j, target in enumerate((q_ref.at[at], k_ref.at[at], v_ref.at[at, pl.ds(0, LANES)])):
            copies.append(pltpu.make_async_copy(ref.at[j], target, in_sems.at[3 * n + j]))
            copies[-1].start()
    v_ref[:, LANES:] = jnp.ones((parts * rows, LANES), BF16)
    docs = doc_ref[...].astype(F32)
    line = lax.broadcasted_iota(jnp.int32, docs.shape, 1)
    used = (line >= DOC_LINE) & (line < DOC_LINE + per)
    starts = [
        jnp.sum(jnp.where(used & (docs < d), 1.0, 0.0)).astype(jnp.int32)
        for d in range(1, LAST_DOC_ID + 1)
    ]
    for copy in copies:
        copy.wait()

    wide = (TILE, LANES)
    lane = lax.broadcasted_iota(jnp.int32, wide, 1)
    sub = lax.broadcasted_iota(jnp.int32, wide, 0)
    step = CHAINS * TILE

    def body(i, carry):
        first = pl.multiple_of(i * step, step)
        low = 0
        for s in starts:
            low = jnp.where(first >= s, s, low)
        count = (i + 1) * CHAINS - low // TILE

        def run(n):
            base = pl.multiple_of(first + step - n * TILE, TILE)
            tops = {}

            def score(chain):
                tiles = n - CHAINS + 1 + chain
                mine = pl.multiple_of(first + chain * TILE, TILE)
                keys = pl.ds(base, tiles * TILE)
                begin = jnp.zeros(wide, jnp.int32)
                for s in starts:
                    begin = jnp.where(sub >= s - mine, s, begin)
                begin = begin - base - lane
                top = jnp.full(wide, MASKED, F32)
                queries = q_ref[pl.ds(mine, TILE), :]
                for c in range(tiles * TILE // LANES):
                    at = head_at(c)
                    if c % 2 == 0:
                        scores = nt_dot(queries, k_ref[pl.ds(pl.multiple_of(base + c * LANES, LANES), 2 * LANES), :])
                    piece = jnp.where(begin <= c * LANES, scores[:, head_at(c % 2)], MASKED)
                    ahead = c * LANES - (tiles - 1) * TILE
                    if ahead >= 0:
                        piece = jnp.where(lane - sub <= -ahead, piece, MASKED)
                    top = jnp.maximum(top, piece)
                    s_ref[chain, :, at] = piece
                tops[chain] = jnp.max(top, axis=1, keepdims=True) * factor

            def mix(chain):
                tiles = n - CHAINS + 1 + chain
                mine = pl.multiple_of(first + chain * TILE, TILE)
                row_max = tops[chain]
                total = jnp.zeros((TILE, 2 * LANES), F32)
                for t in range(tiles):
                    at = slice(t * TILE, (t + 1) * TILE)
                    p = jnp.exp2(s_ref[chain, :, at] * factor - row_max).astype(BF16)
                    keys = pl.ds(pl.multiple_of(base + t * TILE, TILE), TILE)
                    total = total + jnp.dot(p, v_ref[keys, :], preferred_element_type=F32)
                o_ref[pl.ds(mine, TILE), :] = (total[:, :LANES] / total[:, LANES:]).astype(BF16)

            for chain in range(CHAINS):
                score(chain)
            for chain in range(CHAINS):
                mix(chain)

        for n in range(CHAINS, window + CHAINS):
            pl.when(count == n)(functools.partial(run, n))
        at = pl.ds(first, step)
        pltpu.make_async_copy(o_ref.at[at], out_ref.at[at], out_sems.at[i]).start()
        return carry

    blocks = parts * rows // step
    lax.fori_loop(0, blocks, body, 0)
    for i in range(blocks):
        at = pl.ds(i * step, step)
        pltpu.make_async_copy(o_ref.at[at], out_ref.at[at], out_sems.at[i]).wait()


def attend(me, came, docs, order, longest):
    rows = came[0].shape[1]
    tokens = len(order) * rows
    window = min((longest - 1 + TILE - 1) // TILE + 1, tokens // TILE - CHAINS + 1)
    out = jax.ShapeDtypeStruct((tokens, LANES), BF16)
    return pl.pallas_call(
        functools.partial(attend_kernel, order, rows, window),
        in_specs=[pl.BlockSpec(memory_space=pltpu.SMEM)] + [IN_HBM] * len(order) + [IN_VMEM],
        out_specs=IN_HBM,
        out_shape=out,
        scratch_shapes=[
            pltpu.VMEM((tokens, LANES), BF16),
            pltpu.VMEM((tokens, LANES), BF16),
            pltpu.VMEM((tokens, 2 * LANES), BF16),
            pltpu.VMEM((tokens, LANES), BF16),
            pltpu.VMEM((CHAINS, TILE, (window + CHAINS - 1) * TILE), F32),
            pltpu.SemaphoreType.DMA((3 * len(order),)),
            pltpu.SemaphoreType.DMA((tokens // (CHAINS * TILE),)),
        ],
        cost_estimate=pl.CostEstimate(
            flops=2 * tokens * longest * LANES * 2,
            bytes_accessed=moved(*came, out),
            transcendentals=tokens * longest // 2,
        ),
        compiler_params=PARAMS,
        name="attend",
    )(me, *came, docs)


def unpack_kernel(came_ref, out_ref, held_ref, in_sems, out_sems):
    heads, rows = came_ref.shape[0], came_ref.shape[1]
    pieces = rows // LANES
    coming = [
        [
            pltpu.make_async_copy(
                came_ref.at[h, head_at(a)], held_ref.at[head_at(a), head_at(h)], in_sems.at[a, h]
            )
            for h in range(heads)
        ]
        for a in range(pieces)
    ]
    going = [
        pltpu.make_async_copy(held_ref.at[head_at(a)], out_ref.at[head_at(a)], out_sems.at[a])
        for a in range(pieces)
    ]
    for a in range(pieces):
        for copy in coming[a]:
            copy.start()
    for a in range(pieces):
        for copy in coming[a]:
            copy.wait()
        going[a].start()
    for copy in going:
        copy.wait()


def unpack(came):
    heads, rows = came.shape[0], came.shape[1]
    out = jax.ShapeDtypeStruct((rows, heads * LANES), BF16)
    return pl.pallas_call(
        unpack_kernel,
        in_specs=[IN_HBM],
        out_specs=IN_HBM,
        out_shape=out,
        scratch_shapes=[
            pltpu.VMEM(out.shape, BF16),
            pltpu.SemaphoreType.DMA((rows // LANES, heads)),
            pltpu.SemaphoreType.DMA((rows // LANES,)),
        ],
        cost_estimate=pl.CostEstimate(flops=0, bytes_accessed=2 * moved(out), transcendentals=0),
        name="unpack",
    )(came)


def attend_gathered(q, k, v, doc_ids, heads):
    rows = q.shape[0]
    keys = lax.all_gather(k, "ctx", axis=0, tiled=True)
    values = lax.all_gather(v, "ctx", axis=0, tiled=True)
    docs = lax.all_gather(doc_ids, "ctx", axis=0, tiled=True)
    position = lax.axis_index("ctx") * rows + jnp.arange(rows)
    allowed = (jnp.arange(docs.shape[0])[None, :] <= position[:, None]) & (
        docs[None, :] == doc_ids[:, None]
    )

    def one(h):
        queries, head_keys, head_values = (
            lax.dynamic_slice_in_dim(a, h * LANES, LANES, 1) for a in (q, keys, values)
        )
        scores = jnp.where(allowed, nt_dot(queries, head_keys) * LANES ** (-0.5), MASKED)
        weights = jnp.exp(scores - jnp.max(scores, axis=1, keepdims=True))
        mixed = jnp.dot(weights.astype(BF16), head_values, preferred_element_type=F32)
        return (mixed / jnp.sum(weights, axis=1, keepdims=True)).astype(BF16)

    return lax.map(one, jnp.arange(heads)).transpose(1, 0, 2).reshape(rows, heads * LANES)


def local_state_kernel(gate_ref, doc_ref, k_ref, v_ref, out_ref, cum_ref):
    heads, rows = gate_ref.shape
    cumulated = cumulate(gate_ref[...])
    cum_ref[...] = cumulated
    last = cumulated[:, rows - 1 : rows]
    doc = doc_ref[...]
    start, end = doc[:, 0:1], doc[:, rows - 1 : rows]
    weight = jnp.where(doc == end, jnp.exp(last - cumulated), 0.0)
    through = jnp.exp(last) * jnp.where(start == end, 1.0, 0.0)
    line = lax.broadcasted_iota(jnp.int32, (META, LANES), 0)
    common = jnp.where(line == 2, start.astype(F32), jnp.where(line == 3, end.astype(F32), 0.0))
    for a in range(rows // LANES):
        common = jnp.where(line == DOC_LINE + a, doc[:, head_at(a)].astype(F32), common)
    for h in range(heads):
        at = head_at(h)
        turned = jnp.transpose(k_ref[:, at]).astype(F32)
        weighted = (turned * weight[h : h + 1, :]).astype(BF16)
        out_ref[h, :LANES] = jnp.dot(weighted, v_ref[:, at], preferred_element_type=F32).astype(BF16)
        whole = through[h : h + 1, :]
        high = whole.astype(BF16).astype(F32)
        meta = jnp.where(line == 0, high, jnp.where(line == 1, whole - high, common))
        out_ref[h, LANES:] = meta.astype(BF16)


def local_state(k, v, gates, doc_row):
    heads, rows = gates.shape
    outs = [
        jax.ShapeDtypeStruct((heads, LANES + META, LANES), BF16),
        jax.ShapeDtypeStruct((heads, rows), F32),
    ]
    return pl.pallas_call(
        local_state_kernel,
        in_specs=[IN_VMEM] * 4,
        out_specs=[IN_VMEM] * 2,
        out_shape=outs,
        cost_estimate=pl.CostEstimate(
            flops=2 * heads * rows * LANES * LANES,
            bytes_accessed=moved(k, v, gates, *outs),
            transcendentals=heads * rows,
        ),
        compiler_params=PARAMS,
        name="local_state",
    )(gates, doc_row, k, v)


def carry_kernel(came_ref, out_ref, doc_ref, held_ref, sems):
    parts = came_ref.shape[0]
    copies = [pltpu.make_async_copy(came_ref.at[j], held_ref.at[j], sems.at[j]) for j in range(parts)]
    for copy in copies:
        copy.start()
    line = lax.broadcasted_iota(jnp.int32, (META, LANES), 0)
    state = jnp.zeros((LANES, LANES), F32)
    before = jnp.full((1, LANES), -1.0, F32)
    for j in range(parts):
        out_ref[j, :LANES] = state.astype(BF16)
        out_ref[j, LANES:] = jnp.where(line == 3, before, 0.0).astype(BF16)
        copies[j].wait()
        doc_ref[j] = held_ref[j, LANES:]
        meta = held_ref[j, LANES:].astype(F32)
        through = jnp.where(meta[2:3] == before, meta[0:1] + meta[1:2], 0.0)
        state = state * through + held_ref[j, :LANES].astype(F32)
        before = meta[3:4]


def carry(came):
    parts = came.shape[0]
    return pl.pallas_call(
        carry_kernel,
        in_specs=[IN_HBM],
        out_specs=[IN_VMEM] * 2,
        out_shape=[
            jax.ShapeDtypeStruct(came.shape, BF16),
            jax.ShapeDtypeStruct((parts, META, LANES), BF16),
        ],
        scratch_shapes=[pltpu.VMEM(came.shape, BF16), pltpu.SemaphoreType.DMA((came.shape[0],))],
        cost_estimate=pl.CostEstimate(
            flops=2 * came.size, bytes_accessed=2 * moved(came), transcendentals=0
        ),
        compiler_params=PARAMS,
        name="carry",
    )(came)


def carry_gathered(block):
    every = lax.all_gather(block, "ctx")
    state = jnp.zeros(block[:, :LANES].shape, F32)
    before = jnp.full((LANES,), -1.0, F32)

    def one(j, carried):
        state, before = carried
        here = lax.dynamic_index_in_dim(every, j, 0, False).astype(F32)
        meta = here[:, LANES:]
        through = jnp.where(meta[:, 2] == before, meta[:, 0] + meta[:, 1], 0.0)
        return state * through[:, None, :] + here[:, :LANES], meta[0, 3]

    state, before = lax.fori_loop(0, lax.axis_index("ctx"), one, (state, before))
    tail = jnp.zeros((block.shape[0], META, LANES), F32).at[:, 3].set(before)
    return jnp.concatenate([state, tail], axis=1).astype(BF16)


def inside_kernel(cum_ref, doc_ref, q_hbm, k_ref, v_ref, raw_ref, q_ref, sem, column_ref, bias_ref):
    copy = pltpu.make_async_copy(q_hbm, q_ref, sem)
    copy.start()
    heads, rows = cum_ref.shape
    count = rows // LANES
    column_ref[...] = columns(cum_ref[...])
    doc = doc_ref[...].astype(F32)
    square = (LANES, LANES)
    upto = lax.broadcasted_iota(jnp.int32, square, 0) >= lax.broadcasted_iota(jnp.int32, square, 1)
    for a in range(count):
        doc_column = column_of(doc[:, head_at(a)])
        for b in range(a + 1):
            ok = doc_column == doc[:, head_at(b)]
            ok = ok & upto if a == b else ok
            bias_ref[head_at(a), head_at(b)] = jnp.where(ok, 0.0, MASKED)
    copy.wait()
    for h in range(heads):
        at = head_at(h)
        row = cum_ref[h : h + 1, :]
        for a in range(count):
            lines = head_at(a)
            width = (a + 1) * LANES
            scores = nt_dot(q_ref[lines, at], k_ref[0:width, at])
            spread = jnp.concatenate([column_ref[lines, at]] * (a + 1), axis=1) - row[:, :width]
            decayed = scores * jnp.exp(spread + bias_ref[lines, 0:width])
            raw_ref[lines, at] = jnp.dot(
                decayed.astype(BF16), v_ref[0:width, at], preferred_element_type=F32
            )


def inside(q, k, v, cumulated, doc_row):
    heads, rows = cumulated.shape
    out = jax.ShapeDtypeStruct(q.shape, F32)
    return pl.pallas_call(
        inside_kernel,
        in_specs=[IN_VMEM, IN_VMEM, IN_HBM, IN_VMEM, IN_VMEM],
        out_specs=IN_VMEM,
        out_shape=out,
        scratch_shapes=[
            pltpu.VMEM(q.shape, BF16),
            pltpu.SemaphoreType.DMA,
            pltpu.VMEM(q.shape, F32),
            pltpu.VMEM((rows, rows), F32),
        ],
        cost_estimate=pl.CostEstimate(
            flops=3 * heads * rows * rows * LANES,
            bytes_accessed=moved(q, k, v, out),
            transcendentals=heads * rows * rows // 2,
        ),
        compiler_params=PARAMS,
        name="inside",
    )(cumulated, doc_row, q, k, v)


def incoming_kernel(cum_ref, doc_ref, q_hbm, before_ref, raw_ref, out_ref, square_ref, q_ref, sem):
    copy = pltpu.make_async_copy(q_hbm, q_ref, sem)
    copy.start()
    heads, rows = cum_ref.shape
    factor = columns(jnp.exp(cum_ref[...]))
    doc = doc_ref[...].astype(F32)
    meta = before_ref[0, LANES:].astype(F32)
    linked = jnp.concatenate(
        [jnp.where(column_of(doc[:, head_at(a)]) == meta[3:4], 1.0, 0.0) for a in range(rows // LANES)],
        axis=0,
    )
    total = jnp.zeros((rows, LANES), F32)
    copy.wait()
    for h in range(heads):
        at = head_at(h)
        came = jnp.dot(q_ref[:, at], before_ref[h, :LANES], preferred_element_type=F32)
        raw = raw_ref[:, at] + came * (factor[:, at] * linked)
        out_ref[:, at] = raw
        total = total + raw * raw
    square_ref[...] = nt_dot(jnp.ones((8, LANES), F32), total, HIGHEST)


def incoming(q, cumulated, doc_row, before, raw):
    heads, rows = cumulated.shape
    outs = [jax.ShapeDtypeStruct(q.shape, F32), jax.ShapeDtypeStruct((8, rows), F32)]
    return pl.pallas_call(
        incoming_kernel,
        in_specs=[IN_VMEM, IN_VMEM, IN_HBM, IN_VMEM, IN_VMEM],
        out_specs=[IN_VMEM] * 2,
        out_shape=outs,
        scratch_shapes=[pltpu.VMEM(q.shape, BF16), pltpu.SemaphoreType.DMA],
        cost_estimate=pl.CostEstimate(
            flops=2 * heads * rows * LANES * LANES,
            bytes_accessed=moved(q, before, raw, *outs),
            transcendentals=heads * rows,
        ),
        compiler_params=PARAMS,
        name="incoming",
    )(cumulated, doc_row, q, before, raw)


def normalize_kernel(features, raw_ref, gain_ref, *refs):
    *squares, out_ref, made_ref, sems = refs
    total = squares[0][...]
    for ref in squares[1:]:
        total = total + ref[...]
    scale = lax.rsqrt(total / features + EPSILON)
    copies = []
    for a in range(raw_ref.shape[0] // LANES):
        lines = head_at(a)
        column = column_of(scale[0:1, lines])
        for h in range(raw_ref.shape[1] // LANES):
            at = head_at(h)
            made_ref[lines, at] = (raw_ref[lines, at] * column * gain_ref[:, at]).astype(BF16)
        copies.append(pltpu.make_async_copy(made_ref.at[lines], out_ref.at[lines], sems.at[a]))
        copies[-1].start()
    for copy in copies:
        copy.wait()


def normalize(raw, gain_row, squares, features):
    rows, width = raw.shape
    out = jax.ShapeDtypeStruct((rows, width), BF16)
    return pl.pallas_call(
        functools.partial(normalize_kernel, features),
        in_specs=[IN_VMEM] * (2 + len(squares)),
        out_specs=IN_HBM,
        out_shape=out,
        scratch_shapes=[
            pltpu.VMEM((rows, width), BF16),
            pltpu.SemaphoreType.DMA((rows // LANES,)),
        ],
        cost_estimate=pl.CostEstimate(
            flops=3 * raw.size, bytes_accessed=moved(raw, out), transcendentals=rows
        ),
        compiler_params=PARAMS,
        name="normalize",
    )(raw, gain_row, *squares)


def after(x, *earlier):
    return lax.optimization_barrier((x, *earlier))[0]


def exchange(x):
    return lax.all_to_all(x, "ctx", split_axis=0, concat_axis=0, tiled=True)


def on_device(size, head_parts, q_lin, k_lin, v_lin, gate_log, lin_gain, q_soft, k_soft, v_soft, doc_ids):
    heads, rows = gate_log.shape
    doc_row = doc_ids.reshape(1, rows)

    if heads == size and size & (size - 1) == 0:
        me = lax.axis_index("ctx").reshape(1)

        def swap(x, d):
            return lax.ppermute(x, "ctx", [(i, i ^ d) for i in range(size)])

        order = [d for d in range(size - 2, 0, -2)] + [d for d in range(size - 1, 0, -2)] + [0]
        first, second = size // 2 - 1, size // 2 + 1
        sent = pack(me, q_soft, k_soft, v_soft, order)
        came = [swap(x, d) for x, d in zip(sent[:first], order)]
        states, cumulated = local_state(after(k_lin, sent[-1]), v_lin, gate_log, doc_row)
        held_states = exchange(states)
        middle, _ = lax.optimization_barrier((sent[first:second], states))
        came += [swap(x, d) for x, d in zip(middle, order[first:])]
        raw = inside(q_lin, k_lin, v_lin, cumulated, doc_row)
        late, _, held_states = lax.optimization_barrier((sent[second:-1], raw, held_states))
        came += [swap(x, d) for x, d in zip(late, order[second:])]
        passed, docs = carry(held_states)
        before = exchange(passed)
        mixed = attend(me, [*came, sent[-1]], docs, order, rows * size // 2)
        back = exchange(mixed.reshape(size, rows, LANES))
        raw, square = incoming(q_lin, cumulated, doc_row, after(before, mixed), raw)
        soft_out = unpack(back)
    else:
        states, cumulated = local_state(k_lin, v_lin, gate_log, doc_row)
        raw = inside(q_lin, k_lin, v_lin, cumulated, doc_row)
        raw, square = incoming(q_lin, cumulated, doc_row, carry_gathered(states), raw)
        soft_out = attend_gathered(q_soft, k_soft, v_soft, doc_ids, heads)

    squares = [square]
    for d in range(1, head_parts):
        turn = [(i, (i + d) % head_parts) for i in range(head_parts)]
        squares.append(lax.ppermute(square, "head", turn))
    lin_out = normalize(raw, lin_gain.reshape(1, -1), squares, heads * head_parts * LANES)
    return lin_out, soft_out


def solution(mesh):
    split = P("ctx", "head")
    in_specs = (split, split, split, P("head", "ctx"), P("head"), split, split, split, P("ctx"))
    return jax.shard_map(
        functools.partial(on_device, mesh.shape["ctx"], mesh.shape["head"]),
        mesh=mesh,
        in_specs=in_specs,
        out_specs=(split, split),
        check_vma=False,
    )
```

```python
import functools
import math

import jax
import jax.numpy as jnp
from jax import lax
from jax.experimental import pallas as pl
from jax.experimental.pallas import tpu as pltpu
from jax.sharding import PartitionSpec as P

EPSILON = 1e-05
MASKED = -1e30
LANES = 128
META = 16
DOC_LINE = 4
LAST_DOC_ID = 7
TILE = 256
CHAINS = 2
VMEM_MB = 16
F32 = jnp.float32
BF16 = jnp.bfloat16
HIGHEST = lax.Precision.HIGHEST
IN_VMEM = pl.BlockSpec(memory_space=pltpu.VMEM)
IN_HBM = pl.BlockSpec(memory_space=pltpu.HBM)
PARAMS = pltpu.CompilerParams(vmem_limit_bytes=VMEM_MB << 20)


def nt_dot(a, b, precision=None):
    return lax.dot_general(
        a, b, (((1,), (1,)), ((), ())), precision=precision, preferred_element_type=F32
    )


def head_at(h):
    return slice(h * LANES, (h + 1) * LANES)


def column_of(row):
    return jnp.transpose(jnp.broadcast_to(row, (LANES, LANES)))


def three_parts(x):
    a = x.astype(BF16).astype(F32)
    b = (x - a).astype(BF16).astype(F32)
    return a, b, x - a - b


def cumulate(gates):
    heads, rows = gates.shape
    lower = lax.broadcasted_iota(jnp.int32, (rows, rows), 0) <= lax.broadcasted_iota(
        jnp.int32, (rows, rows), 1
    )
    parts = jnp.concatenate([*three_parts(gates), jnp.zeros_like(gates)], axis=0).astype(BF16)
    sums = jnp.dot(parts, jnp.where(lower, 1.0, 0.0).astype(BF16), preferred_element_type=F32)
    return sums[:heads] + sums[heads : 2 * heads] + sums[2 * heads : 3 * heads]


def columns(x):
    heads, rows = x.shape
    filler = jnp.zeros((LANES - 3 * heads, rows), F32)
    parts = jnp.concatenate([*three_parts(x), filler], axis=0)
    turned = jnp.concatenate(
        [jnp.transpose(parts[:, head_at(a)]) for a in range(rows // LANES)], axis=0
    ).astype(BF16)
    line = lax.broadcasted_iota(jnp.int32, (LANES, heads * LANES), 0)
    lane = lax.broadcasted_iota(jnp.int32, (LANES, heads * LANES), 1)
    pick = (line < 3 * heads) & (lax.rem(line, heads) == lane // LANES)
    return jnp.dot(turned, jnp.where(pick, 1.0, 0.0).astype(BF16), preferred_element_type=F32)


def moved(*shapes):
    return sum(math.prod(s.shape) * jnp.dtype(s.dtype).itemsize for s in shapes)


def pack_kernel(order, me_ref, *refs):
    ins, outs, (held_ref, in_sems, out_sems) = refs[:3], refs[3:-3], refs[-3:]
    coming, going = [], []
    for n, d in enumerate(order):
        lanes = pl.ds(pl.multiple_of(lax.bitwise_xor(me_ref[0], d) * LANES, LANES), LANES)
        for i, ref in enumerate(ins):
            coming.append(
                pltpu.make_async_copy(ref.at[:, lanes], held_ref.at[n, i], in_sems.at[3 * n + i])
            )
            coming[-1].start()
    for n, out_ref in enumerate(outs):
        for copy in coming[3 * n : 3 * n + 3]:
            copy.wait()
        going.append(pltpu.make_async_copy(held_ref.at[n], out_ref, out_sems.at[n]))
        going[-1].start()
    for copy in going:
        copy.wait()


def pack(me, q, k, v, order):
    rows = q.shape[0]
    n = len(order)
    outs = [jax.ShapeDtypeStruct((3, rows, LANES), BF16)] * n
    return pl.pallas_call(
        functools.partial(pack_kernel, order),
        in_specs=[pl.BlockSpec(memory_space=pltpu.SMEM)] + [IN_HBM] * 3,
        out_specs=[IN_HBM] * n,
        out_shape=outs,
        scratch_shapes=[
            pltpu.VMEM((n, 3, rows, LANES), BF16),
            pltpu.SemaphoreType.DMA((3 * n,)),
            pltpu.SemaphoreType.DMA((n,)),
        ],
        cost_estimate=pl.CostEstimate(flops=0, bytes_accessed=2 * moved(*outs), transcendentals=0),
        name="pack",
    )(me, q, k, v)


def attend_kernel(order, rows, window, me_ref, *refs):
    came = refs[: len(order)]
    doc_ref, out_ref, q_ref, k_ref, v_ref, o_ref, s_ref, in_sems, out_sems = refs[len(order) :]
    parts = len(order)
    per = rows // LANES
    factor = LANES ** (-0.5) * math.log2(math.e)
    copies = []
    for n, (d, ref) in enumerate(zip(order, came)):
        at = pl.ds(pl.multiple_of(lax.bitwise_xor(me_ref[0], d) * rows, LANES), rows)
        for j, target in enumerate((q_ref.at[at], k_ref.at[at], v_ref.at[at, pl.ds(0, LANES)])):
            copies.append(pltpu.make_async_copy(ref.at[j], target, in_sems.at[3 * n + j]))
            copies[-1].start()
    v_ref[:, LANES:] = jnp.ones((parts * rows, LANES), BF16)
    docs = doc_ref[...].astype(F32)
    line = lax.broadcasted_iota(jnp.int32, docs.shape, 1)
    used = (line >= DOC_LINE) & (line < DOC_LINE + per)
    starts = [
        jnp.sum(jnp.where(used & (docs < d), 1.0, 0.0)).astype(jnp.int32)
        for d in range(1, LAST_DOC_ID + 1)
    ]
    for copy in copies:
        copy.wait()

    wide = (TILE, LANES)
    lane = lax.broadcasted_iota(jnp.int32, wide, 1)
    sub = lax.broadcasted_iota(jnp.int32, wide, 0)
    step = CHAINS * TILE

    def body(i, carry):
        first = pl.multiple_of(i * step, step)
        low, low_next = 0, 0
        for s in starts:
            low = jnp.where(first >= s, s, low)
            low_next = jnp.where(first + TILE >= s, s, low_next)
        count = (i + 1) * CHAINS - low // TILE

        def run(counts):
            tops = {}

            def score(chain):
                tiles = counts[chain]
                mine = pl.multiple_of(first + chain * TILE, TILE)
                base = pl.multiple_of(mine + TILE - tiles * TILE, TILE)
                begin = jnp.zeros(wide, jnp.int32)
                for s in starts:
                    begin = jnp.where(sub >= s - mine, s, begin)
                begin = begin - base - lane
                top = jnp.full(wide, MASKED, F32)
                queries = q_ref[pl.ds(mine, TILE), :]
                for c in range(tiles * TILE // LANES):
                    at = head_at(c)
                    if c % 2 == 0:
                        scores = nt_dot(queries, k_ref[pl.ds(pl.multiple_of(base + c * LANES, LANES), 2 * LANES), :])
                    piece = jnp.where(begin <= c * LANES, scores[:, head_at(c % 2)], MASKED)
                    ahead = c * LANES - (tiles - 1) * TILE
                    if ahead >= 0:
                        piece = jnp.where(lane - sub <= -ahead, piece, MASKED)
                    top = jnp.maximum(top, piece)
                    s_ref[chain, :, at] = piece
                tops[chain] = jnp.max(top, axis=1, keepdims=True) * factor

            def mix(chain):
                tiles = counts[chain]
                mine = pl.multiple_of(first + chain * TILE, TILE)
                base = pl.multiple_of(mine + TILE - tiles * TILE, TILE)
                row_max = tops[chain]
                total = jnp.zeros((TILE, 2 * LANES), F32)
                for t in range(tiles):
                    at = slice(t * TILE, (t + 1) * TILE)
                    p = jnp.exp2(s_ref[chain, :, at] * factor - row_max).astype(BF16)
                    keys = pl.ds(pl.multiple_of(base + t * TILE, TILE), TILE)
                    total = total + jnp.dot(p, v_ref[keys, :], preferred_element_type=F32)
                o_ref[pl.ds(mine, TILE), :] = (total[:, :LANES] / total[:, LANES:]).astype(BF16)

            for chain in range(CHAINS):
                score(chain)
            for chain in range(CHAINS):
                mix(chain)

        for n in range(2, window + 2):
            if n < 4:
                pl.when(count == n)(functools.partial(run, (n - 1, n)))
            else:
                pl.when((count == n) & (low == low_next))(functools.partial(run, (n - 1, n)))
                pl.when((count == n) & (low != low_next))(functools.partial(run, (n - 1, 2)))
        at = pl.ds(first, step)
        pltpu.make_async_copy(o_ref.at[at], out_ref.at[at], out_sems.at[i]).start()
        return carry

    blocks = parts * rows // step
    lax.fori_loop(0, blocks, body, 0)
    for i in range(blocks):
        at = pl.ds(i * step, step)
        pltpu.make_async_copy(o_ref.at[at], out_ref.at[at], out_sems.at[i]).wait()


def attend(me, came, docs, order, longest):
    rows = came[0].shape[1]
    tokens = len(order) * rows
    window = min((longest - 1 + TILE - 1) // TILE + 1, tokens // TILE - CHAINS + 1)
    out = jax.ShapeDtypeStruct((tokens, LANES), BF16)
    return pl.pallas_call(
        functools.partial(attend_kernel, order, rows, window),
        in_specs=[pl.BlockSpec(memory_space=pltpu.SMEM)] + [IN_HBM] * len(order) + [IN_VMEM],
        out_specs=IN_HBM,
        out_shape=out,
        scratch_shapes=[
            pltpu.VMEM((tokens, LANES), BF16),
            pltpu.VMEM((tokens, LANES), BF16),
            pltpu.VMEM((tokens, 2 * LANES), BF16),
            pltpu.VMEM((tokens, LANES), BF16),
            pltpu.VMEM((CHAINS, TILE, (window + CHAINS - 1) * TILE), F32),
            pltpu.SemaphoreType.DMA((3 * len(order),)),
            pltpu.SemaphoreType.DMA((tokens // (CHAINS * TILE),)),
        ],
        cost_estimate=pl.CostEstimate(
            flops=2 * tokens * longest * LANES * 2,
            bytes_accessed=moved(*came, out),
            transcendentals=tokens * longest // 2,
        ),
        compiler_params=PARAMS,
        name="attend",
    )(me, *came, docs)


def unpack_kernel(came_ref, out_ref, held_ref, in_sems, out_sems):
    heads, rows = came_ref.shape[0], came_ref.shape[1]
    pieces = rows // LANES
    coming = [
        [
            pltpu.make_async_copy(
                came_ref.at[h, head_at(a)], held_ref.at[head_at(a), head_at(h)], in_sems.at[a, h]
            )
            for h in range(heads)
        ]
        for a in range(pieces)
    ]
    going = [
        pltpu.make_async_copy(held_ref.at[head_at(a)], out_ref.at[head_at(a)], out_sems.at[a])
        for a in range(pieces)
    ]
    for a in range(pieces):
        for copy in coming[a]:
            copy.start()
    for a in range(pieces):
        for copy in coming[a]:
            copy.wait()
        going[a].start()
    for copy in going:
        copy.wait()


def unpack(came):
    heads, rows = came.shape[0], came.shape[1]
    out = jax.ShapeDtypeStruct((rows, heads * LANES), BF16)
    return pl.pallas_call(
        unpack_kernel,
        in_specs=[IN_HBM],
        out_specs=IN_HBM,
        out_shape=out,
        scratch_shapes=[
            pltpu.VMEM(out.shape, BF16),
            pltpu.SemaphoreType.DMA((rows // LANES, heads)),
            pltpu.SemaphoreType.DMA((rows // LANES,)),
        ],
        cost_estimate=pl.CostEstimate(flops=0, bytes_accessed=2 * moved(out), transcendentals=0),
        name="unpack",
    )(came)


def attend_gathered(q, k, v, doc_ids, heads):
    rows = q.shape[0]
    keys = lax.all_gather(k, "ctx", axis=0, tiled=True)
    values = lax.all_gather(v, "ctx", axis=0, tiled=True)
    docs = lax.all_gather(doc_ids, "ctx", axis=0, tiled=True)
    position = lax.axis_index("ctx") * rows + jnp.arange(rows)
    allowed = (jnp.arange(docs.shape[0])[None, :] <= position[:, None]) & (
        docs[None, :] == doc_ids[:, None]
    )

    def one(h):
        queries, head_keys, head_values = (
            lax.dynamic_slice_in_dim(a, h * LANES, LANES, 1) for a in (q, keys, values)
        )
        scores = jnp.where(allowed, nt_dot(queries, head_keys) * LANES ** (-0.5), MASKED)
        weights = jnp.exp(scores - jnp.max(scores, axis=1, keepdims=True))
        mixed = jnp.dot(weights.astype(BF16), head_values, preferred_element_type=F32)
        return (mixed / jnp.sum(weights, axis=1, keepdims=True)).astype(BF16)

    return lax.map(one, jnp.arange(heads)).transpose(1, 0, 2).reshape(rows, heads * LANES)


def local_state_kernel(gate_ref, doc_ref, k_ref, v_ref, out_ref, cum_ref):
    heads, rows = gate_ref.shape
    cumulated = cumulate(gate_ref[...])
    cum_ref[...] = cumulated
    last = cumulated[:, rows - 1 : rows]
    doc = doc_ref[...]
    start, end = doc[:, 0:1], doc[:, rows - 1 : rows]
    weight = jnp.where(doc == end, jnp.exp(last - cumulated), 0.0)
    through = jnp.exp(last) * jnp.where(start == end, 1.0, 0.0)
    line = lax.broadcasted_iota(jnp.int32, (META, LANES), 0)
    common = jnp.where(line == 2, start.astype(F32), jnp.where(line == 3, end.astype(F32), 0.0))
    for a in range(rows // LANES):
        common = jnp.where(line == DOC_LINE + a, doc[:, head_at(a)].astype(F32), common)
    for h in range(heads):
        at = head_at(h)
        turned = jnp.transpose(k_ref[:, at]).astype(F32)
        weighted = (turned * weight[h : h + 1, :]).astype(BF16)
        out_ref[h, :LANES] = jnp.dot(weighted, v_ref[:, at], preferred_element_type=F32).astype(BF16)
        whole = through[h : h + 1, :]
        high = whole.astype(BF16).astype(F32)
        meta = jnp.where(line == 0, high, jnp.where(line == 1, whole - high, common))
        out_ref[h, LANES:] = meta.astype(BF16)


def local_state(k, v, gates, doc_row):
    heads, rows = gates.shape
    outs = [
        jax.ShapeDtypeStruct((heads, LANES + META, LANES), BF16),
        jax.ShapeDtypeStruct((heads, rows), F32),
    ]
    return pl.pallas_call(
        local_state_kernel,
        in_specs=[IN_VMEM] * 4,
        out_specs=[IN_VMEM] * 2,
        out_shape=outs,
        cost_estimate=pl.CostEstimate(
            flops=2 * heads * rows * LANES * LANES,
            bytes_accessed=moved(k, v, gates, *outs),
            transcendentals=heads * rows,
        ),
        compiler_params=PARAMS,
        name="local_state",
    )(gates, doc_row, k, v)


def carry_kernel(came_ref, out_ref, doc_ref, held_ref, sems):
    parts = came_ref.shape[0]
    copies = [pltpu.make_async_copy(came_ref.at[j], held_ref.at[j], sems.at[j]) for j in range(parts)]
    for copy in copies:
        copy.start()
    line = lax.broadcasted_iota(jnp.int32, (META, LANES), 0)
    state = jnp.zeros((LANES, LANES), F32)
    before = jnp.full((1, LANES), -1.0, F32)
    for j in range(parts):
        out_ref[j, :LANES] = state.astype(BF16)
        out_ref[j, LANES:] = jnp.where(line == 3, before, 0.0).astype(BF16)
        copies[j].wait()
        doc_ref[j] = held_ref[j, LANES:]
        meta = held_ref[j, LANES:].astype(F32)
        through = jnp.where(meta[2:3] == before, meta[0:1] + meta[1:2], 0.0)
        state = state * through + held_ref[j, :LANES].astype(F32)
        before = meta[3:4]


def carry(came):
    parts = came.shape[0]
    return pl.pallas_call(
        carry_kernel,
        in_specs=[IN_HBM],
        out_specs=[IN_VMEM] * 2,
        out_shape=[
            jax.ShapeDtypeStruct(came.shape, BF16),
            jax.ShapeDtypeStruct((parts, META, LANES), BF16),
        ],
        scratch_shapes=[pltpu.VMEM(came.shape, BF16), pltpu.SemaphoreType.DMA((came.shape[0],))],
        cost_estimate=pl.CostEstimate(
            flops=2 * came.size, bytes_accessed=2 * moved(came), transcendentals=0
        ),
        compiler_params=PARAMS,
        name="carry",
    )(came)


def carry_gathered(block):
    every = lax.all_gather(block, "ctx")
    state = jnp.zeros(block[:, :LANES].shape, F32)
    before = jnp.full((LANES,), -1.0, F32)

    def one(j, carried):
        state, before = carried
        here = lax.dynamic_index_in_dim(every, j, 0, False).astype(F32)
        meta = here[:, LANES:]
        through = jnp.where(meta[:, 2] == before, meta[:, 0] + meta[:, 1], 0.0)
        return state * through[:, None, :] + here[:, :LANES], meta[0, 3]

    state, before = lax.fori_loop(0, lax.axis_index("ctx"), one, (state, before))
    tail = jnp.zeros((block.shape[0], META, LANES), F32).at[:, 3].set(before)
    return jnp.concatenate([state, tail], axis=1).astype(BF16)


def inside_kernel(cum_ref, doc_ref, q_hbm, k_ref, v_ref, raw_ref, q_ref, sem, column_ref, bias_ref):
    copy = pltpu.make_async_copy(q_hbm, q_ref, sem)
    copy.start()
    heads, rows = cum_ref.shape
    count = rows // LANES
    column_ref[...] = columns(cum_ref[...])
    doc = doc_ref[...].astype(F32)
    square = (LANES, LANES)
    upto = lax.broadcasted_iota(jnp.int32, square, 0) >= lax.broadcasted_iota(jnp.int32, square, 1)
    for a in range(count):
        doc_column = column_of(doc[:, head_at(a)])
        for b in range(a + 1):
            ok = doc_column == doc[:, head_at(b)]
            ok = ok & upto if a == b else ok
            bias_ref[head_at(a), head_at(b)] = jnp.where(ok, 0.0, MASKED)
    copy.wait()
    for h in range(heads):
        at = head_at(h)
        row = cum_ref[h : h + 1, :]
        for a in range(count):
            lines = head_at(a)
            width = (a + 1) * LANES
            scores = nt_dot(q_ref[lines, at], k_ref[0:width, at])
            spread = jnp.concatenate([column_ref[lines, at]] * (a + 1), axis=1) - row[:, :width]
            decayed = scores * jnp.exp(spread + bias_ref[lines, 0:width])
            raw_ref[lines, at] = jnp.dot(
                decayed.astype(BF16), v_ref[0:width, at], preferred_element_type=F32
            )


def inside(q, k, v, cumulated, doc_row):
    heads, rows = cumulated.shape
    out = jax.ShapeDtypeStruct(q.shape, F32)
    return pl.pallas_call(
        inside_kernel,
        in_specs=[IN_VMEM, IN_VMEM, IN_HBM, IN_VMEM, IN_VMEM],
        out_specs=IN_VMEM,
        out_shape=out,
        scratch_shapes=[
            pltpu.VMEM(q.shape, BF16),
            pltpu.SemaphoreType.DMA,
            pltpu.VMEM(q.shape, F32),
            pltpu.VMEM((rows, rows), F32),
        ],
        cost_estimate=pl.CostEstimate(
            flops=3 * heads * rows * rows * LANES,
            bytes_accessed=moved(q, k, v, out),
            transcendentals=heads * rows * rows // 2,
        ),
        compiler_params=PARAMS,
        name="inside",
    )(cumulated, doc_row, q, k, v)


def incoming_kernel(cum_ref, doc_ref, q_hbm, before_ref, raw_ref, out_ref, square_ref, q_ref, sem):
    copy = pltpu.make_async_copy(q_hbm, q_ref, sem)
    copy.start()
    heads, rows = cum_ref.shape
    factor = columns(jnp.exp(cum_ref[...]))
    doc = doc_ref[...].astype(F32)
    meta = before_ref[0, LANES:].astype(F32)
    linked = jnp.concatenate(
        [jnp.where(column_of(doc[:, head_at(a)]) == meta[3:4], 1.0, 0.0) for a in range(rows // LANES)],
        axis=0,
    )
    total = jnp.zeros((rows, LANES), F32)
    copy.wait()
    for h in range(heads):
        at = head_at(h)
        came = jnp.dot(q_ref[:, at], before_ref[h, :LANES], preferred_element_type=F32)
        raw = raw_ref[:, at] + came * (factor[:, at] * linked)
        out_ref[:, at] = raw
        total = total + raw * raw
    square_ref[...] = nt_dot(jnp.ones((8, LANES), F32), total, HIGHEST)


def incoming(q, cumulated, doc_row, before, raw):
    heads, rows = cumulated.shape
    outs = [jax.ShapeDtypeStruct(q.shape, F32), jax.ShapeDtypeStruct((8, rows), F32)]
    return pl.pallas_call(
        incoming_kernel,
        in_specs=[IN_VMEM, IN_VMEM, IN_HBM, IN_VMEM, IN_VMEM],
        out_specs=[IN_VMEM] * 2,
        out_shape=outs,
        scratch_shapes=[pltpu.VMEM(q.shape, BF16), pltpu.SemaphoreType.DMA],
        cost_estimate=pl.CostEstimate(
            flops=2 * heads * rows * LANES * LANES,
            bytes_accessed=moved(q, before, raw, *outs),
            transcendentals=heads * rows,
        ),
        compiler_params=PARAMS,
        name="incoming",
    )(cumulated, doc_row, q, before, raw)


def normalize_kernel(features, raw_ref, gain_ref, *refs):
    *squares, out_ref, made_ref, sems = refs
    total = squares[0][...]
    for ref in squares[1:]:
        total = total + ref[...]
    scale = lax.rsqrt(total / features + EPSILON)
    copies = []
    for a in range(raw_ref.shape[0] // LANES):
        lines = head_at(a)
        column = column_of(scale[0:1, lines])
        for h in range(raw_ref.shape[1] // LANES):
            at = head_at(h)
            made_ref[lines, at] = (raw_ref[lines, at] * column * gain_ref[:, at]).astype(BF16)
        copies.append(pltpu.make_async_copy(made_ref.at[lines], out_ref.at[lines], sems.at[a]))
        copies[-1].start()
    for copy in copies:
        copy.wait()


def normalize(raw, gain_row, squares, features):
    rows, width = raw.shape
    out = jax.ShapeDtypeStruct((rows, width), BF16)
    return pl.pallas_call(
        functools.partial(normalize_kernel, features),
        in_specs=[IN_VMEM] * (2 + len(squares)),
        out_specs=IN_HBM,
        out_shape=out,
        scratch_shapes=[
            pltpu.VMEM((rows, width), BF16),
            pltpu.SemaphoreType.DMA((rows // LANES,)),
        ],
        cost_estimate=pl.CostEstimate(
            flops=3 * raw.size, bytes_accessed=moved(raw, out), transcendentals=rows
        ),
        compiler_params=PARAMS,
        name="normalize",
    )(raw, gain_row, *squares)


def after(x, *earlier):
    return lax.optimization_barrier((x, *earlier))[0]


def exchange(x):
    return lax.all_to_all(x, "ctx", split_axis=0, concat_axis=0, tiled=True)


def on_device(size, head_parts, q_lin, k_lin, v_lin, gate_log, lin_gain, q_soft, k_soft, v_soft, doc_ids):
    heads, rows = gate_log.shape
    doc_row = doc_ids.reshape(1, rows)

    if heads == size and size & (size - 1) == 0:
        me = lax.axis_index("ctx").reshape(1)

        def swap(x, d):
            return lax.ppermute(x, "ctx", [(i, i ^ d) for i in range(size)])

        order = [d for d in range(size - 2, 0, -2)] + [d for d in range(size - 1, 0, -2)] + [0]
        first, second = size // 2 - 1, size // 2 + 1
        sent = pack(me, q_soft, k_soft, v_soft, order)
        came = [swap(x, d) for x, d in zip(sent[:first], order)]
        states, cumulated = local_state(after(k_lin, sent[-1]), v_lin, gate_log, doc_row)
        held_states = exchange(states)
        middle, _ = lax.optimization_barrier((sent[first:second], states))
        came += [swap(x, d) for x, d in zip(middle, order[first:])]
        raw = inside(q_lin, k_lin, v_lin, cumulated, doc_row)
        late, _, held_states = lax.optimization_barrier((sent[second:-1], raw, held_states))
        came += [swap(x, d) for x, d in zip(late, order[second:])]
        passed, docs = carry(held_states)
        before = exchange(passed)
        mixed = attend(me, [*came, sent[-1]], docs, order, rows * size // 2)
        back = exchange(mixed.reshape(size, rows, LANES))
        raw, square = incoming(q_lin, cumulated, doc_row, after(before, mixed), raw)
        soft_out = unpack(back)
    else:
        states, cumulated = local_state(k_lin, v_lin, gate_log, doc_row)
        raw = inside(q_lin, k_lin, v_lin, cumulated, doc_row)
        raw, square = incoming(q_lin, cumulated, doc_row, carry_gathered(states), raw)
        soft_out = attend_gathered(q_soft, k_soft, v_soft, doc_ids, heads)

    squares = [square]
    for d in range(1, head_parts):
        turn = [(i, (i + d) % head_parts) for i in range(head_parts)]
        squares.append(lax.ppermute(square, "head", turn))
    lin_out = normalize(raw, lin_gain.reshape(1, -1), squares, heads * head_parts * LANES)
    return lin_out, soft_out


def solution(mesh):
    split = P("ctx", "head")
    in_specs = (split, split, split, P("head", "ctx"), P("head"), split, split, split, P("ctx"))
    return jax.shard_map(
        functools.partial(on_device, mesh.shape["ctx"], mesh.shape["head"]),
        mesh=mesh,
        in_specs=in_specs,
        out_specs=(split, split),
        check_vma=False,
    )
```
